32 devices in a mesh: pairs: 8 (over z, y), dom: 4 (over x, core).
Axes of the slice: x: 2, y: 2, z: 4, core: 2. Of those that a mesh axis runs over, the one named last changes fastest.
Arguments:
- amplitude: bfloat16 [64, 384, 384], P('pairs', 'dom'), may hold values from -2 to 2
- integrals: bfloat16 [64, 384, 384], P('pairs', 'dom'), may hold values from -6 to 6
- virtual_energy: float32 [64, 384], P('pairs'), may hold values from 0.2 to 1.5
- occupied_gap: float32 [64], P('pairs'), may hold values from 0.3 to 1.5
- pair_slot: int32 [64], replicated, may hold values from 0 to 63, as said below
- coupling_source: int32 [128], replicated, may hold values from 0 to 63, as said below
- coupling_target: int32 [128], replicated, may hold values from 0 to 63, as said below
- coupling_fock: float32 [128], P(('pairs', 'dom')), may hold values from -3 to 3
- coupling_intersection: bfloat16 [128, 384, 384], P(('pairs', 'dom')), may hold values from -0.3125 to 0.3125
Outputs:
- updated_amplitude: float32 [64, 384, 384], P('pairs', 'dom')
- residual: float32 [64, 384, 384], P('pairs', 'dom')
The draws below stay inside these ranges and needn't reach their ends.
Inputs may be any that keep to these rules, and one draw needn't show every extreme that they name: A permutation: pair p is stored at position pair_slot[p], which lies on index pair_slot[p] // 8 of pairs. `coupling_target`: coupling c is held by index c // 16 of pairs, and its target pair is stored on that same index; the two couplings that share a source pair on one holder have different targets. `coupling_source`: among the 16 couplings of one holder, every source pair appears in exactly two, and there are 8 distinct source pairs; of the pairs stored on any one index of pairs, a holder uses at most 2 distinct ones as sources, and exactly 2 for some indices on every holder.
All inputs are finite; a program needn't handle non-finite values.
Results may differ from the reference program's by a relative error of at most 0.0024.
Values may be sent and summed in bfloat16 or wider, within the bound.
A program may use at most 128 MiB of HBM per device.

```python
import math
import jax
import jax.numpy as jnp
from jax import lax

W = 384
PAIR_DEV = 8
UPDATES = 1
PAIRS = 64
CPL_DEV = 16
COUPLINGS = 128
N_DOM = 4


def shuffle_rows(keys, length):

    def one_row(row_key):
        return jax.random.permutation(row_key, length)
    return jax.vmap(one_row)(keys).astype(jnp.int32)


def coupling_tables(key):
    base = jax.random.fold_in(key, 7101)
    keys = jax.random.split(base, 8)
    holders = PAIRS // PAIR_DEV
    doubled = 3 * holders // 8
    single = holders // 4
    pair_slot = jax.random.permutation(keys[0], PAIRS).astype(jnp.int32)
    slot_pair = jnp.argsort(pair_slot).astype(jnp.int32)
    owner_order = shuffle_rows(jax.random.split(keys[1], holders), holders)
    twice = owner_order[:, :doubled]
    once = owner_order[:, doubled:doubled + single]
    first_local = jax.random.randint(keys[2], (holders, doubled), 0, PAIR_DEV)
    second_local = (first_local + 1 + jax.random.randint(keys[3], (holders, doubled), 0, PAIR_DEV - 1)) % PAIR_DEV
    once_local = jax.random.randint(keys[4], (holders, single), 0, PAIR_DEV)
    owners = jnp.concatenate([twice, twice, once], axis=1)
    local_index = jnp.concatenate([first_local, second_local, once_local], axis=1)
    sources = owners * PAIR_DEV + local_index
    first_target = jax.random.randint(keys[5], sources.shape, 0, PAIR_DEV)
    second_target = (first_target + 1 + jax.random.randint(keys[6], sources.shape, 0, PAIR_DEV - 1)) % PAIR_DEV
    holder_base = jnp.arange(holders, dtype=jnp.int32)[:, None] * PAIR_DEV
    source_all = jnp.concatenate([sources, sources], axis=1)
    target_all = jnp.concatenate([first_target, second_target], axis=1) + holder_base
    shuffle = shuffle_rows(jax.random.split(keys[7], holders), CPL_DEV)
    source_all = jnp.take_along_axis(source_all, shuffle, axis=1).reshape(-1)
    target_all = jnp.take_along_axis(target_all, shuffle, axis=1).reshape(-1)
    return (pair_slot, jnp.take(slot_pair, source_all).astype(jnp.int32), jnp.take(slot_pair, target_all).astype(jnp.int32))


def draw_pair_slot(key, part):
    return coupling_tables(key)[0]


def draw_coupling_source(key, part):
    return coupling_tables(key)[1]


def draw_coupling_target(key, part):
    return coupling_tables(key)[2]


def steps_of(key, shape, shards, low, high):
    level = 1.0
    for position, shards_of in shards:
        draws = jax.random.uniform(jax.random.fold_in(jax.random.fold_in(key, 6), position), (shards_of,), jnp.float32, low / len(shards), high / len(shards))
        level = level * jnp.repeat(jnp.exp(draws), shape[position] // shards_of).reshape((-1,) + (1,) * (len(shape) - 1 - position))
    return level


def gaussian(stream_key, dims, spread, most, shards=(), kind=jnp.bfloat16):
    entries = spread * jax.random.normal(stream_key, dims, jnp.float32)
    if shards:
        entries = entries * steps_of(stream_key, dims, shards, -0.22, 0.18)
    return jnp.clip(entries, -most, most).astype(kind)


def setup_inputs(seed: int = 0) -> dict:
    key_of = jax.random.split(jax.random.key(seed), 10)
    return {
        "amplitude": gaussian(key_of[0], (PAIRS, W, W), 0.3, 2.0, ((0, 8), (1, 4))),
        "integrals": gaussian(key_of[1], (PAIRS, W, W), 1.0, 6.0, ((0, 8), (1, 4))),
        "virtual_energy": jnp.clip(jnp.exp(math.log(1.5) - 2.014903 * jax.random.uniform(key_of[2], (PAIRS, W), jnp.float32) ** steps_of(key_of[2], (PAIRS, W), ((0, 8),), -0.2, 0.2)), 0.2, 1.5),
        "occupied_gap": jnp.clip(jnp.exp(math.log(1.5) - 1.60943787 * jax.random.uniform(key_of[3], (PAIRS,), jnp.float32) ** steps_of(key_of[3], (PAIRS,), ((0, 8),), -0.2, 0.2)), 0.3, 1.5),
        "pair_slot": draw_pair_slot(jax.random.fold_in(key_of[9], 71), 0),
        "coupling_source": draw_coupling_source(jax.random.fold_in(key_of[9], 71), 0),
        "coupling_target": draw_coupling_target(jax.random.fold_in(key_of[9], 71), 0),
        "coupling_fock": gaussian(key_of[7], (COUPLINGS,), 0.5, 3.0, ((0, 32),), jnp.float32),
        "coupling_intersection": gaussian(key_of[8], (COUPLINGS, W, W), W ** -0.5, 0.3125, ((0, 32),)),
    }


def reference(amplitude, integrals, virtual_energy, occupied_gap, pair_slot, coupling_source, coupling_target, coupling_fock, coupling_intersection):
    source_slot = jnp.take(pair_slot, coupling_source).astype(jnp.int32)
    target_slot = jnp.take(pair_slot, coupling_target).astype(jnp.int32)
    denominator = virtual_energy[:, :, None] + virtual_energy[:, None, :] + occupied_gap[:, None, None]
    current = amplitude.astype(jnp.float32)
    block = CPL_DEV // N_DOM
    blocks = COUPLINGS // block
    residual = jnp.zeros(current.shape, jnp.float32)
    for step in range(UPDATES):
        sent = current.astype(jnp.bfloat16)

        def add_block(total, index):
            start = (index * block).astype(jnp.int32)
            sources = lax.dynamic_slice_in_dim(source_slot, start, block)
            targets = lax.dynamic_slice_in_dim(target_slot, start, block)
            fock = lax.dynamic_slice_in_dim(coupling_fock, start, block)
            intersection = lax.dynamic_slice_in_dim(coupling_intersection, start, block).astype(jnp.float32)
            picked = jnp.take(sent, sources, axis=0).astype(jnp.float32)
            left = jnp.einsum("cab,cbd->cad", intersection, picked).astype(jnp.bfloat16)
            left = lax.optimization_barrier(left).astype(jnp.float32)
            projected = jnp.einsum("cad,ced->cae", left, intersection)
            coupled_term = (fock[:, None, None] * projected).astype(jnp.bfloat16)
            coupled_term = lax.optimization_barrier(coupled_term).astype(jnp.float32)
            return total.at[targets].add(coupled_term), None

        coupled, unused = lax.scan(add_block, jnp.zeros(current.shape, jnp.float32), jnp.arange(blocks, dtype=jnp.int32))
        residual = integrals.astype(jnp.float32) + denominator * current - coupled
        current = current - residual / denominator
    return current, residual
```

```python
import jax
import jax.numpy as jnp
from jax import lax
from jax.sharding import PartitionSpec as P

SRC_CAP = 2


def lookup(table, indices):
    places = jnp.arange(table.shape[0], dtype=jnp.int32)
    return jnp.sum(jnp.where(indices[:, None] == places[None, :], table[None, :], 0), axis=1)


def per_device(
    amplitude,
    integrals,
    virtual_energy,
    occupied_gap,
    pair_slot,
    coupling_source,
    coupling_target,
    coupling_fock,
    coupling_intersection,
):
    holders = lax.axis_size("pairs")
    quarters = lax.axis_size("dom")
    own_pair = lax.axis_index("pairs")
    own_quarter = lax.axis_index("dom")
    pair_count, row_count, width = amplitude.shape
    couplings = coupling_source.shape[0] // holders
    quarter_couplings = coupling_intersection.shape[0]
    source_slot = lookup(pair_slot, coupling_source).reshape(holders, couplings)
    target_slot = lookup(pair_slot, coupling_target).reshape(holders, couplings)
    source_owner = source_slot // pair_count
    source_local = source_slot % pair_count
    held_owner = lax.dynamic_index_in_dim(source_owner, own_pair, 0, keepdims=False)
    held_local = lax.dynamic_index_in_dim(source_local, own_pair, 0, keepdims=False)
    held_target = lax.dynamic_index_in_dim(target_slot, own_pair, 0, keepdims=False) % pair_count
    local_numbers = jnp.arange(pair_count, dtype=jnp.int32)
    owner_numbers = jnp.arange(holders, dtype=jnp.int32)
    capacity = SRC_CAP
    wanted = jnp.any(
        (source_owner[:, :, None] == own_pair)
        & (source_local[:, :, None] == local_numbers[None, None, :]),
        axis=1,
    )
    wanted_count = wanted.astype(jnp.int32)
    order = jnp.cumsum(wanted_count, axis=1) - wanted_count
    slot_numbers = jnp.arange(capacity, dtype=jnp.int32)
    chosen = wanted[:, None, :] & (order[:, None, :] == slot_numbers[None, :, None])
    picked = jnp.sum(jnp.where(chosen, local_numbers[None, None, :], 0), axis=2)
    match = (held_owner[:, None, None] == owner_numbers[None, :, None]) & (
        held_local[:, None, None] == local_numbers[None, None, :]
    )
    needed = jnp.any(match, axis=0).astype(jnp.int32)
    held_order = jnp.cumsum(needed, axis=1) - needed
    held_rank = jnp.sum(jnp.where(match, held_order[None], 0), axis=(1, 2))
    held_slot = held_owner * capacity + held_rank
    energy_rows = lax.dynamic_slice_in_dim(virtual_energy, own_quarter * row_count, row_count, 1)
    denominator = energy_rows[:, :, None] + virtual_energy[:, None, :] + occupied_gap[:, None, None]
    target_select = (held_target[None, :] == local_numbers[:, None]).astype(jnp.bfloat16)
    current = amplitude.astype(jnp.float32)
    sent = current.astype(jnp.bfloat16)
    outgoing = jnp.take(sent, picked.reshape(-1), axis=0).reshape(
        holders, capacity, row_count, width
    )
    arrived = lax.all_to_all(outgoing, "pairs", split_axis=0, concat_axis=0, tiled=True)
    held_rows = jnp.take(arrived.reshape(holders * capacity, row_count, width), held_slot, axis=0)
    grouped = held_rows.reshape(quarters, quarter_couplings, row_count, width)
    whole = lax.all_to_all(grouped, "dom", split_axis=0, concat_axis=2, tiled=True).reshape(
        quarter_couplings, quarters * row_count, width
    )
    left = jnp.einsum(
        "cab,cbd->cad", coupling_intersection, whole, preferred_element_type=jnp.float32
    ).astype(jnp.bfloat16)
    projected = jnp.einsum(
        "cad,ced->cae", left, coupling_intersection, preferred_element_type=jnp.float32
    )
    coupled_term = (coupling_fock[:, None, None] * projected).astype(jnp.bfloat16)
    scattered = lax.all_to_all(
        coupled_term.reshape(quarter_couplings, quarters, row_count, width),
        "dom",
        split_axis=1,
        concat_axis=0,
        tiled=True,
    ).reshape(couplings, row_count, width)
    coupled = jnp.einsum(
        "pc,crd->prd", target_select, scattered, preferred_element_type=jnp.float32
    )
    residual = integrals.astype(jnp.float32) + denominator * current - coupled
    current = current - residual / denominator
    return (current, residual)


def solution(mesh):
    in_specs = (
        P("pairs", "dom", None),
        P("pairs", "dom", None),
        P("pairs", None),
        P("pairs"),
        P(),
        P(),
        P(),
        P(("pairs", "dom")),
        P(("pairs", "dom"), None, None),
    )
    out_specs = (P("pairs", "dom", None), P("pairs", "dom", None))
    return jax.shard_map(
        per_device, mesh=mesh, in_specs=in_specs, out_specs=out_specs, check_vma=False
    )
```

```python
import functools

import jax
import jax.numpy as jnp
from jax import lax
from jax.experimental import pallas as pl
from jax.experimental.pallas import tpu as pltpu
from jax.sharding import PartitionSpec as P

SRC_CAP = 2
CHUNKS = 2
MESH = pl.DeviceIdType.MESH
VMEM = pltpu.VMEM
SMEM = pltpu.SMEM


def prepare_kernel(
    holders, slot_ref, source_ref, target_ref, amp_ref, out_ref, held_ref, local_ref, first_ref
):
    me = lax.axis_index("pairs")
    pair_count = amp_ref.shape[0]
    couplings = source_ref.shape[0] // holders
    base = me * pair_count
    unroll = 8 if couplings % 8 == 0 else 1

    def holder_step(h, carry):
        def block(i, ab):
            first, second = ab
            for u in range(unroll):
                local = slot_ref[source_ref[h * couplings + i * unroll + u]] - base
                mine = (local >= 0) & (local < pair_count)
                free = first < 0
                second = jnp.where(mine & jnp.logical_not(free) & (local != first), local, second)
                first = jnp.where(mine & free, local, first)
            return first, second

        first, second = lax.fori_loop(
            0, couplings // unroll, block, (jnp.int32(-1), jnp.int32(-1))
        )
        out_ref[h * SRC_CAP] = amp_ref[jnp.maximum(first, 0)]
        out_ref[h * SRC_CAP + 1] = amp_ref[jnp.maximum(second, 0)]
        return carry

    lax.fori_loop(0, holders, holder_step, 0)

    def clear(i, carry):
        first_ref[i] = jnp.int32(-1)
        return carry

    lax.fori_loop(0, holders, clear, 0)

    def own_step(c, carry):
        slot = slot_ref[source_ref[me * couplings + c]]
        owner = lax.div(slot, jnp.int32(pair_count))
        local = slot - owner * pair_count
        known = first_ref[owner]
        first_ref[owner] = jnp.where(known < 0, local, known)
        rank = jnp.where((known < 0) | (known == local), 0, 1)
        held_ref[c] = owner * SRC_CAP + rank
        local_ref[c] = slot_ref[target_ref[me * couplings + c]] - base
        return carry

    lax.fori_loop(0, couplings, own_step, 0)


def exchange_kernel(
    holders,
    quarters,
    held_ref,
    fock_ref,
    out_ref,
    inter_ref,
    terms_ref,
    whole,
    picked,
    sent_terms,
    send1,
    recv1,
    local1,
    send2,
    recv2,
    send3,
    recv3,
    local3,
    *arrived,
):
    me = lax.axis_index("pairs")
    quarter = lax.axis_index("dom")
    chunks = len(arrived)
    slots, chunk_rows, width = arrived[0].shape
    rows = chunk_rows * chunks
    group = inter_ref.shape[0]
    half = holders // 2
    my_half = me // half
    in_half = me % half

    barrier = pltpu.get_barrier_semaphore()

    def greet(j, carry):
        pl.semaphore_signal(
            barrier, inc=1, device_id=((me + j) % holders, quarter), device_id_type=MESH
        )
        return carry

    lax.fori_loop(1, holders, greet, 0)
    for d in range(1, quarters):
        pl.semaphore_signal(
            barrier, inc=1, device_id=(me, (quarter + d) % quarters), device_id_type=MESH
        )
    pl.semaphore_wait(barrier, holders - 1 + quarters - 1)

    def owner_copy(k, h):
        span = pl.ds(k * chunk_rows, chunk_rows)
        return pltpu.make_async_remote_copy(
            src_ref=out_ref.at[pl.ds(h * SRC_CAP, SRC_CAP), span],
            dst_ref=arrived[k].at[pl.ds(me * SRC_CAP, SRC_CAP)],
            send_sem=send1.at[k, h],
            recv_sem=recv1.at[k, me],
            device_id=(h, quarter),
            device_id_type=MESH,
        )

    def arrival(k, h):
        span = pl.ds(k * chunk_rows, chunk_rows)
        return pltpu.make_async_remote_copy(
            src_ref=out_ref.at[pl.ds(h * SRC_CAP, SRC_CAP), span],
            dst_ref=arrived[k].at[pl.ds(h * SRC_CAP, SRC_CAP)],
            send_sem=send1.at[k, h],
            recv_sem=recv1.at[k, h],
            device_id=(h, quarter),
            device_id_type=MESH,
        )

    def own_copy(k):
        span = pl.ds(k * chunk_rows, chunk_rows)
        return pltpu.make_async_copy(
            out_ref.at[pl.ds(me * SRC_CAP, SRC_CAP), span],
            arrived[k].at[pl.ds(me * SRC_CAP, SRC_CAP)],
            local1.at[k],
        )

    for k in range(chunks):

        def far(j, carry, k=k):
            owner_copy(k, (1 - my_half) * half + (in_half + j) % half).start()
            return carry

        def near(j, carry, k=k):
            owner_copy(k, my_half * half + (in_half + j) % half).start()
            return carry

        lax.fori_loop(0, half, far, 0)
        lax.fori_loop(1, half, near, 0)
        own_copy(k).start()

    def peer_copy(k, d):
        peer = (quarter + d) % quarters
        return pltpu.make_async_remote_copy(
            src_ref=picked.at[d - 1, k],
            dst_ref=whole.at[:, pl.ds(pl.multiple_of(quarter * rows + k * chunk_rows, 16), chunk_rows)],
            send_sem=send2.at[k, d],
            recv_sem=recv2.at[k, d],
            device_id=(me, peer),
            device_id_type=MESH,
        )

    def peer_arrival(k, d):
        peer = (quarter + quarters - d) % quarters
        return pltpu.make_async_remote_copy(
            src_ref=picked.at[d - 1, k],
            dst_ref=whole.at[:, pl.ds(pl.multiple_of(peer * rows + k * chunk_rows, 16), chunk_rows)],
            send_sem=send2.at[k, d],
            recv_sem=recv2.at[k, d],
            device_id=(me, peer),
            device_id_type=MESH,
        )

    for k in range(chunks):

        def take(j, carry, k=k):
            arrival(k, (me + j) % holders).wait_recv()
            return carry

        lax.fori_loop(1, holders, take, 0)
        own_copy(k).wait()
        for d in range(1, quarters):
            peer = (quarter + d) % quarters

            def pick(c, carry, k=k, d=d, peer=peer):
                picked[d - 1, k, c] = arrived[k][held_ref[peer * group + c]]
                return carry

            lax.fori_loop(0, group, pick, 0)

        for d in range(1, quarters):
            peer_copy(k, d).start()

        def keep(c, carry, k=k):
            start = pl.multiple_of(quarter * rows + k * chunk_rows, 16)
            whole[c, pl.ds(start, chunk_rows)] = arrived[k][held_ref[quarter * group + c]]
            return carry

        lax.fori_loop(0, group, keep, 0)

    for k in range(chunks):
        for d in range(1, quarters):
            peer_arrival(k, d).wait_recv()

    def term_copy(c, d):
        peer = (quarter + d) % quarters
        return pltpu.make_async_remote_copy(
            src_ref=sent_terms.at[c, pl.ds(pl.multiple_of(peer * rows, 16), rows)],
            dst_ref=terms_ref.at[quarter * group + c],
            send_sem=send3.at[c, d],
            recv_sem=recv3.at[c, d],
            device_id=(me, peer),
            device_id_type=MESH,
        )

    def term_arrival(c, d):
        peer = (quarter + quarters - d) % quarters
        return pltpu.make_async_remote_copy(
            src_ref=sent_terms.at[c, pl.ds(pl.multiple_of(peer * rows, 16), rows)],
            dst_ref=terms_ref.at[peer * group + c],
            send_sem=send3.at[c, d],
            recv_sem=recv3.at[c, d],
            device_id=(me, peer),
            device_id_type=MESH,
        )

    def own_term(c):
        return pltpu.make_async_copy(
            sent_terms.at[c, pl.ds(pl.multiple_of(quarter * rows, 16), rows)],
            terms_ref.at[quarter * group + c],
            local3.at[c],
        )

    def multiply(c, carry):
        inter = inter_ref[c]
        left = jnp.dot(inter, whole[c], preferred_element_type=jnp.float32).astype(jnp.bfloat16)
        projected = lax.dot_general(
            left, inter, (((1,), (1,)), ((), ())), preferred_element_type=jnp.float32
        )
        sent_terms[c] = (fock_ref[c] * projected).astype(jnp.bfloat16)
        for d in range(1, quarters):
            term_copy(c, d).start()
        own_term(c).start()
        return carry

    lax.fori_loop(0, group, multiply, 0)

    def finish(c, carry):
        for d in range(1, quarters):
            term_arrival(c, d).wait_recv()
        for d in range(1, quarters):
            term_copy(c, d).wait_send()
        own_term(c).wait()
        return carry

    lax.fori_loop(0, group, finish, 0)
    for k in range(chunks):

        def sent(j, carry, k=k):
            owner_copy(k, (me + j) % holders).wait_send()
            return carry

        lax.fori_loop(1, holders, sent, 0)
        for d in range(1, quarters):
            peer_copy(k, d).wait_send()


def update_kernel(
    local_ref, gap_ref, terms_ref, amp_ref, integrals_ref, rows_ref, energy_ref, new_ref, residual_ref
):
    p = pl.program_id(0)
    couplings = terms_ref.shape[0]
    residual_ref[0] = jnp.zeros_like(residual_ref[0])
    for c in range(couplings):

        @pl.when(local_ref[c] == p)
        def _():
            residual_ref[0] += terms_ref[c].astype(jnp.float32)

    current = amp_ref[0].astype(jnp.float32)
    denominator = rows_ref[0] + energy_ref[0] + gap_ref[p]
    residual = integrals_ref[0].astype(jnp.float32) + denominator * current - residual_ref[0]
    residual_ref[0] = residual
    new_ref[0] = current - residual / denominator


def per_device(
    amplitude,
    integrals,
    virtual_energy,
    occupied_gap,
    pair_slot,
    coupling_source,
    coupling_target,
    coupling_fock,
    coupling_intersection,
):
    holders = lax.axis_size("pairs")
    quarters = lax.axis_size("dom")
    own_quarter = lax.axis_index("dom")
    pair_count, rows, width = amplitude.shape
    couplings = coupling_source.shape[0] // holders
    group = coupling_intersection.shape[0]
    slots = holders * SRC_CAP
    chunks = CHUNKS
    chunk_rows = rows // chunks
    bf16 = jnp.bfloat16
    in_vmem = pl.BlockSpec(memory_space=VMEM)
    in_smem = pl.BlockSpec(memory_space=SMEM)
    anywhere = pl.BlockSpec(memory_space=pl.ANY)

    outgoing, held, local = pl.pallas_call(
        functools.partial(prepare_kernel, holders),
        out_shape=(
            jax.ShapeDtypeStruct((slots, rows, width), bf16),
            jax.ShapeDtypeStruct((couplings,), jnp.int32),
            jax.ShapeDtypeStruct((couplings,), jnp.int32),
        ),
        in_specs=[in_smem, in_smem, in_smem, in_vmem],
        out_specs=(in_vmem, in_smem, in_smem),
        scratch_shapes=[SMEM((holders,), jnp.int32)],
        name="prepare",
    )(pair_slot, coupling_source, coupling_target, amplitude)

    dma = pltpu.SemaphoreType.DMA
    terms = pl.pallas_call(
        functools.partial(exchange_kernel, holders, quarters),
        out_shape=jax.ShapeDtypeStruct((couplings, rows, width), bf16),
        in_specs=[in_smem, in_smem, anywhere, in_vmem],
        out_specs=anywhere,
        scratch_shapes=[
            VMEM((group, quarters * rows, width), bf16),
            VMEM((quarters - 1, chunks, group, chunk_rows, width), bf16),
            VMEM((group, quarters * rows, width), bf16),
            dma((chunks, holders)),
            dma((chunks, holders)),
            dma((chunks,)),
            dma((chunks, quarters)),
            dma((chunks, quarters)),
            dma((group, quarters)),
            dma((group, quarters)),
            dma((group,)),
        ]
        + [VMEM((slots, chunk_rows, width), bf16)] * chunks,
        compiler_params=pltpu.CompilerParams(
            collective_id=0, has_side_effects=True, vmem_limit_bytes=60 << 20
        ),
        name="exchange",
    )(held, coupling_fock, outgoing, coupling_intersection)

    energy_rows = lax.dynamic_slice_in_dim(virtual_energy, own_quarter * rows, rows, 1)
    block = pl.BlockSpec((1, rows, width), lambda p, *_: (p, 0, 0))
    return pl.pallas_call(
        update_kernel,
        out_shape=(
            jax.ShapeDtypeStruct((pair_count, rows, width), jnp.float32),
            jax.ShapeDtypeStruct((pair_count, rows, width), jnp.float32),
        ),
        grid_spec=pltpu.PrefetchScalarGridSpec(
            num_scalar_prefetch=2,
            grid=(pair_count,),
            in_specs=[
                pl.BlockSpec(
                    (couplings, rows, width), lambda p, *_: (0, 0, 0), pipeline_mode=pl.Buffered(1)
                ),
                block,
                block,
                pl.BlockSpec((1, rows, 1), lambda p, *_: (p, 0, 0)),
                pl.BlockSpec((1, 1, width), lambda p, *_: (p, 0, 0)),
            ],
            out_specs=(block, block),
        ),
        name="update",
    )(
        local,
        occupied_gap,
        terms,
        amplitude,
        integrals,
        energy_rows[:, :, None],
        virtual_energy[:, None, :],
    )


def solution(mesh):
    in_specs = (
        P("pairs", "dom", None),
        P("pairs", "dom", None),
        P("pairs", None),
        P("pairs"),
        P(),
        P(),
        P(),
        P(("pairs", "dom")),
        P(("pairs", "dom"), None, None),
    )
    out_specs = (P("pairs", "dom", None), P("pairs", "dom", None))
    return jax.shard_map(
        per_device, mesh=mesh, in_specs=in_specs, out_specs=out_specs, check_vma=False
    )
```

```python
import functools

import jax
import jax.numpy as jnp
from jax import lax
from jax.experimental import pallas as pl
from jax.experimental.pallas import tpu as pltpu
from jax.sharding import PartitionSpec as P

SRC_CAP = 2
CHUNK_ROWS = 16
MESH = pl.DeviceIdType.MESH
VMEM = pltpu.VMEM
SMEM = pltpu.SMEM


def prepare_kernel(
    holders, slot_ref, source_ref, target_ref, amp_ref, out_ref, held_ref, local_ref, first_ref
):
    me = lax.axis_index("pairs")
    pair_count = amp_ref.shape[0]
    couplings = source_ref.shape[0] // holders
    base = me * pair_count
    unroll = 8 if couplings % 8 == 0 else 1

    def holder_step(h, carry):
        def block(i, ab):
            first, second = ab
            for u in range(unroll):
                local = slot_ref[source_ref[h * couplings + i * unroll + u]] - base
                mine = (local >= 0) & (local < pair_count)
                free = first < 0
                second = jnp.where(mine & jnp.logical_not(free) & (local != first), local, second)
                first = jnp.where(mine & free, local, first)
            return first, second

        first, second = lax.fori_loop(
            0, couplings // unroll, block, (jnp.int32(-1), jnp.int32(-1))
        )
        out_ref[h * SRC_CAP] = amp_ref[jnp.maximum(first, 0)]
        out_ref[h * SRC_CAP + 1] = amp_ref[jnp.maximum(second, 0)]
        return carry

    lax.fori_loop(0, holders, holder_step, 0)

    def clear(i, carry):
        first_ref[i] = jnp.int32(-1)
        return carry

    lax.fori_loop(0, holders, clear, 0)

    def own_step(c, carry):
        slot = slot_ref[source_ref[me * couplings + c]]
        owner = lax.div(slot, jnp.int32(pair_count))
        local = slot - owner * pair_count
        known = first_ref[owner]
        first_ref[owner] = jnp.where(known < 0, local, known)
        rank = jnp.where((known < 0) | (known == local), 0, 1)
        held_ref[c] = owner * SRC_CAP + rank
        local_ref[c] = slot_ref[target_ref[me * couplings + c]] - base
        return carry

    lax.fori_loop(0, couplings, own_step, 0)


def exchange_kernel(
    holders,
    quarters,
    held_ref,
    fock_ref,
    out_ref,
    inter_ref,
    terms_ref,
    whole,
    picked,
    sent_terms,
    send1,
    recv1,
    local1,
    send2,
    recv2,
    send3,
    recv3,
    local3,
    *arrived,
):
    me = lax.axis_index("pairs")
    quarter = lax.axis_index("dom")
    chunks = len(arrived)
    slots, chunk_rows, width = arrived[0].shape
    rows = chunk_rows * chunks
    group = inter_ref.shape[0]
    half = holders // 2
    my_half = me // half
    in_half = me % half

    barrier = pltpu.get_barrier_semaphore()

    def greet(j, carry):
        pl.semaphore_signal(
            barrier, inc=1, device_id=((me + j) % holders, quarter), device_id_type=MESH
        )
        return carry

    lax.fori_loop(1, holders, greet, 0)
    for d in range(1, quarters):
        pl.semaphore_signal(
            barrier, inc=1, device_id=(me, (quarter + d) % quarters), device_id_type=MESH
        )
    pl.semaphore_wait(barrier, holders - 1 + quarters - 1)

    def owner_copy(k, h):
        span = pl.ds(k * chunk_rows, chunk_rows)
        return pltpu.make_async_remote_copy(
            src_ref=out_ref.at[pl.ds(h * SRC_CAP, SRC_CAP), span],
            dst_ref=arrived[k].at[pl.ds(me * SRC_CAP, SRC_CAP)],
            send_sem=send1.at[k, h],
            recv_sem=recv1.at[k, me],
            device_id=(h, quarter),
            device_id_type=MESH,
        )

    def arrival(k, h):
        span = pl.ds(k * chunk_rows, chunk_rows)
        return pltpu.make_async_remote_copy(
            src_ref=out_ref.at[pl.ds(h * SRC_CAP, SRC_CAP), span],
            dst_ref=arrived[k].at[pl.ds(h * SRC_CAP, SRC_CAP)],
            send_sem=send1.at[k, h],
            recv_sem=recv1.at[k, h],
            device_id=(h, quarter),
            device_id_type=MESH,
        )

    def own_copy(k):
        span = pl.ds(k * chunk_rows, chunk_rows)
        return pltpu.make_async_copy(
            out_ref.at[pl.ds(me * SRC_CAP, SRC_CAP), span],
            arrived[k].at[pl.ds(me * SRC_CAP, SRC_CAP)],
            local1.at[k],
        )

    for k in range(chunks):

        def far(j, carry, k=k):
            owner_copy(k, (1 - my_half) * half + (in_half + j) % half).start()
            return carry

        def near(j, carry, k=k):
            owner_copy(k, my_half * half + (in_half + j) % half).start()
            return carry

        lax.fori_loop(0, half, far, 0)
        lax.fori_loop(1, half, near, 0)
        own_copy(k).start()

    def peer_copy(k, d):
        peer = (quarter + d) % quarters
        return pltpu.make_async_remote_copy(
            src_ref=picked.at[d - 1, k],
            dst_ref=whole.at[:, pl.ds(pl.multiple_of(quarter * rows + k * chunk_rows, 16), chunk_rows)],
            send_sem=send2.at[k, d],
            recv_sem=recv2.at[k, d],
            device_id=(me, peer),
            device_id_type=MESH,
        )

    def peer_arrival(k, d):
        peer = (quarter + quarters - d) % quarters
        return pltpu.make_async_remote_copy(
            src_ref=picked.at[d - 1, k],
            dst_ref=whole.at[:, pl.ds(pl.multiple_of(peer * rows + k * chunk_rows, 16), chunk_rows)],
            send_sem=send2.at[k, d],
            recv_sem=recv2.at[k, d],
            device_id=(me, peer),
            device_id_type=MESH,
        )

    for k in range(chunks):

        def take(j, carry, k=k):
            arrival(k, (me + j) % holders).wait_recv()
            return carry

        lax.fori_loop(1, holders, take, 0)
        own_copy(k).wait()
        for d in range(1, quarters):
            peer = (quarter + d) % quarters

            def pick(c, carry, k=k, d=d, peer=peer):
                picked[d - 1, k, c] = arrived[k][held_ref[peer * group + c]]
                return carry

            lax.fori_loop(0, group, pick, 0)

        for d in range(1, quarters):
            peer_copy(k, d).start()

        def keep(c, carry, k=k):
            start = pl.multiple_of(quarter * rows + k * chunk_rows, 16)
            whole[c, pl.ds(start, chunk_rows)] = arrived[k][held_ref[quarter * group + c]]
            return carry

        lax.fori_loop(0, group, keep, 0)

    for k in range(chunks):
        for d in range(1, quarters):
            peer_arrival(k, d).wait_recv()

    def term_copy(c, d):
        peer = (quarter + d) % quarters
        return pltpu.make_async_remote_copy(
            src_ref=sent_terms.at[c, pl.ds(pl.multiple_of(peer * rows, 16), rows)],
            dst_ref=terms_ref.at[quarter * group + c],
            send_sem=send3.at[c, d],
            recv_sem=recv3.at[c, d],
            device_id=(me, peer),
            device_id_type=MESH,
        )

    def term_arrival(c, d):
        peer = (quarter + quarters - d) % quarters
        return pltpu.make_async_remote_copy(
            src_ref=sent_terms.at[c, pl.ds(pl.multiple_of(peer * rows, 16), rows)],
            dst_ref=terms_ref.at[peer * group + c],
            send_sem=send3.at[c, d],
            recv_sem=recv3.at[c, d],
            device_id=(me, peer),
            device_id_type=MESH,
        )

    def own_term(c):
        return pltpu.make_async_copy(
            sent_terms.at[c, pl.ds(pl.multiple_of(quarter * rows, 16), rows)],
            terms_ref.at[quarter * group + c],
            local3.at[c],
        )

    def multiply(c, carry):
        inter = inter_ref[c]
        left = jnp.dot(inter, whole[c], preferred_element_type=jnp.float32).astype(jnp.bfloat16)
        projected = lax.dot_general(
            left, inter, (((1,), (1,)), ((), ())), preferred_element_type=jnp.float32
        )
        sent_terms[c] = (fock_ref[c] * projected).astype(jnp.bfloat16)
        for d in range(1, quarters):
            term_copy(c, d).start()
        own_term(c).start()
        return carry

    lax.fori_loop(0, group, multiply, 0)

    def finish(c, carry):
        for d in range(1, quarters):
            term_arrival(c, d).wait_recv()
        for d in range(1, quarters):
            term_copy(c, d).wait_send()
        own_term(c).wait()
        return carry

    lax.fori_loop(0, group, finish, 0)
    for k in range(chunks):

        def sent(j, carry, k=k):
            owner_copy(k, (me + j) % holders).wait_send()
            return carry

        lax.fori_loop(1, holders, sent, 0)
        for d in range(1, quarters):
            peer_copy(k, d).wait_send()


def update_kernel(
    local_ref,
    gap_ref,
    terms_hbm,
    amp_hbm,
    integrals_hbm,
    energy_ref,
    new_hbm,
    residual_hbm,
    terms,
    amp,
    integrals,
    new,
    residual,
    columns,
    term_sem,
    in_sem,
    out_sem,
):
    quarter = lax.axis_index("dom")
    couplings = terms.shape[0]
    pair_count, rows, width = amp.shape

    def term_copy(c):
        return pltpu.make_async_copy(terms_hbm.at[c], terms.at[c], term_sem.at[c])

    def in_copies(p):
        return (
            pltpu.make_async_copy(amp_hbm.at[p], amp.at[p], in_sem.at[0, p]),
            pltpu.make_async_copy(integrals_hbm.at[p], integrals.at[p], in_sem.at[1, p]),
        )

    def out_copies(p):
        return (
            pltpu.make_async_copy(new.at[p], new_hbm.at[p], out_sem.at[0, p]),
            pltpu.make_async_copy(residual.at[p], residual_hbm.at[p], out_sem.at[1, p]),
        )

    def start_term(c, carry):
        term_copy(c).start()
        return carry

    lax.fori_loop(0, couplings, start_term, 0)
    for p in range(pair_count):
        for copy in in_copies(p):
            copy.start()
    columns[...] = jnp.transpose(energy_ref[...])
    residual[...] = jnp.zeros_like(residual)

    def add_term(c, carry):
        term_copy(c).wait()
        p = local_ref[c]
        residual[p] = residual[p] + terms[c].astype(jnp.float32)
        return carry

    lax.fori_loop(0, couplings, add_term, 0)
    own_rows = columns[pl.ds(pl.multiple_of(quarter * rows, 8), rows), :]
    for p in range(pair_count):
        for copy in in_copies(p):
            copy.wait()
        current = amp[p].astype(jnp.float32)
        denominator = own_rows[:, p : p + 1] + energy_ref[p : p + 1, :] + gap_ref[p]
        rest = integrals[p].astype(jnp.float32) + denominator * current - residual[p]
        residual[p] = rest
        new[p] = current - rest / denominator
        for copy in out_copies(p):
            copy.start()
    for p in range(pair_count):
        for copy in out_copies(p):
            copy.wait()


def per_device(
    amplitude,
    integrals,
    virtual_energy,
    occupied_gap,
    pair_slot,
    coupling_source,
    coupling_target,
    coupling_fock,
    coupling_intersection,
):
    holders = lax.axis_size("pairs")
    quarters = lax.axis_size("dom")
    own_quarter = lax.axis_index("dom")
    pair_count, rows, width = amplitude.shape
    couplings = coupling_source.shape[0] // holders
    group = coupling_intersection.shape[0]
    slots = holders * SRC_CAP
    chunk_rows = CHUNK_ROWS if rows % CHUNK_ROWS == 0 else rows
    chunks = rows // chunk_rows
    bf16 = jnp.bfloat16
    in_vmem = pl.BlockSpec(memory_space=VMEM)
    in_smem = pl.BlockSpec(memory_space=SMEM)
    anywhere = pl.BlockSpec(memory_space=pl.ANY)

    outgoing, held, local = pl.pallas_call(
        functools.partial(prepare_kernel, holders),
        out_shape=(
            jax.ShapeDtypeStruct((slots, rows, width), bf16),
            jax.ShapeDtypeStruct((couplings,), jnp.int32),
            jax.ShapeDtypeStruct((couplings,), jnp.int32),
        ),
        in_specs=[in_smem, in_smem, in_smem, in_vmem],
        out_specs=(in_vmem, in_smem, in_smem),
        scratch_shapes=[SMEM((holders,), jnp.int32)],
        name="prepare",
    )(pair_slot, coupling_source, coupling_target, amplitude)

    dma = pltpu.SemaphoreType.DMA
    terms = pl.pallas_call(
        functools.partial(exchange_kernel, holders, quarters),
        out_shape=jax.ShapeDtypeStruct((couplings, rows, width), bf16),
        in_specs=[in_smem, in_smem, anywhere, in_vmem],
        out_specs=anywhere,
        scratch_shapes=[
            VMEM((group, quarters * rows, width), bf16),
            VMEM((quarters - 1, chunks, group, chunk_rows, width), bf16),
            VMEM((group, quarters * rows, width), bf16),
            dma((chunks, holders)),
            dma((chunks, holders)),
            dma((chunks,)),
            dma((chunks, quarters)),
            dma((chunks, quarters)),
            dma((group, quarters)),
            dma((group, quarters)),
            dma((group,)),
        ]
        + [VMEM((slots, chunk_rows, width), bf16)] * chunks,
        compiler_params=pltpu.CompilerParams(
            collective_id=0, has_side_effects=True, vmem_limit_bytes=60 << 20
        ),
        name="exchange",
    )(held, coupling_fock, outgoing, coupling_intersection)

    out = jax.ShapeDtypeStruct((pair_count, rows, width), jnp.float32)
    return pl.pallas_call(
        update_kernel,
        out_shape=(out, out),
        in_specs=[in_smem, in_smem, anywhere, anywhere, anywhere, in_vmem],
        out_specs=(anywhere, anywhere),
        scratch_shapes=[
            VMEM((couplings, rows, width), bf16),
            VMEM((pair_count, rows, width), bf16),
            VMEM((pair_count, rows, width), bf16),
            VMEM((pair_count, rows, width), jnp.float32),
            VMEM((pair_count, rows, width), jnp.float32),
            VMEM((width, pair_count), jnp.float32),
            dma((couplings,)),
            dma((2, pair_count)),
            dma((2, pair_count)),
        ],
        name="update",
    )(local, occupied_gap, terms, amplitude, integrals, virtual_energy)


def solution(mesh):
    in_specs = (
        P("pairs", "dom", None),
        P("pairs", "dom", None),
        P("pairs", None),
        P("pairs"),
        P(),
        P(),
        P(),
        P(("pairs", "dom")),
        P(("pairs", "dom"), None, None),
    )
    out_specs = (P("pairs", "dom", None), P("pairs", "dom", None))
    return jax.shard_map(
        per_device, mesh=mesh, in_specs=in_specs, out_specs=out_specs, check_vma=False
    )
```

```python
import functools

import jax
import jax.numpy as jnp
from jax import lax
from jax.experimental import pallas as pl
from jax.experimental.pallas import tpu as pltpu
from jax.sharding import PartitionSpec as P

SRC_CAP = 2
CHUNK_ROWS = 16
MESH = pl.DeviceIdType.MESH
VMEM = pltpu.VMEM
SMEM = pltpu.SMEM


def exchange_kernel(
    holders,
    quarters,
    slot_ref,
    source_ref,
    target_ref,
    fock_ref,
    amp_ref,
    inter_hbm,
    terms_ref,
    local_ref,
    out_ref,
    inter_ref,
    held_ref,
    inter_sem,
    whole,
    picked,
    sent_terms,
    send1,
    recv1,
    local1,
    send2,
    recv2,
    send3,
    recv3,
    local3,
    *arrived,
):
    me = lax.axis_index("pairs")
    quarter = lax.axis_index("dom")
    chunks = len(arrived)
    slots, chunk_rows, width = arrived[0].shape
    rows = chunk_rows * chunks
    group = inter_hbm.shape[0]
    half = holders // 2
    my_half = me // half
    in_half = me % half

    barrier = pltpu.get_barrier_semaphore()

    def greet(j, carry):
        pl.semaphore_signal(
            barrier, inc=1, device_id=((me + j) % holders, quarter), device_id_type=MESH
        )
        return carry

    lax.fori_loop(1, holders, greet, 0)
    for d in range(1, quarters):
        pl.semaphore_signal(
            barrier, inc=1, device_id=(me, (quarter + d) % quarters), device_id_type=MESH
        )

    def inter_copy(c):
        return pltpu.make_async_copy(inter_hbm.at[c], inter_ref.at[c], inter_sem.at[c])

    def fetch(c, carry):
        inter_copy(c).start()
        return carry

    lax.fori_loop(0, group, fetch, 0)

    pair_count = amp_ref.shape[0]
    couplings = source_ref.shape[0] // holders
    base = me * pair_count
    unroll = 8 if couplings % 8 == 0 else 1

    def holder_step(h, carry):
        def block(i, ab):
            first, second = ab
            for u in range(unroll):
                local = slot_ref[source_ref[h * couplings + i * unroll + u]] - base
                mine = (local >= 0) & (local < pair_count)
                free = first < 0
                second = jnp.where(mine & jnp.logical_not(free) & (local != first), local, second)
                first = jnp.where(mine & free, local, first)
            return first, second

        first, second = lax.fori_loop(
            0, couplings // unroll, block, (jnp.int32(-1), jnp.int32(-1))
        )
        out_ref[h * SRC_CAP] = amp_ref[jnp.maximum(first, 0)]
        out_ref[h * SRC_CAP + 1] = amp_ref[jnp.maximum(second, 0)]
        return carry

    lax.fori_loop(0, holders, holder_step, 0)
    pl.semaphore_wait(barrier, holders - 1 + quarters - 1)

    def owner_copy(k, h):
        span = pl.ds(k * chunk_rows, chunk_rows)
        return pltpu.make_async_remote_copy(
            src_ref=out_ref.at[pl.ds(h * SRC_CAP, SRC_CAP), span],
            dst_ref=arrived[k].at[pl.ds(me * SRC_CAP, SRC_CAP)],
            send_sem=send1.at[k, h],
            recv_sem=recv1.at[k, me],
            device_id=(h, quarter),
            device_id_type=MESH,
        )

    def arrival(k, h):
        span = pl.ds(k * chunk_rows, chunk_rows)
        return pltpu.make_async_remote_copy(
            src_ref=out_ref.at[pl.ds(h * SRC_CAP, SRC_CAP), span],
            dst_ref=arrived[k].at[pl.ds(h * SRC_CAP, SRC_CAP)],
            send_sem=send1.at[k, h],
            recv_sem=recv1.at[k, h],
            device_id=(h, quarter),
            device_id_type=MESH,
        )

    def own_copy(k):
        span = pl.ds(k * chunk_rows, chunk_rows)
        return pltpu.make_async_copy(
            out_ref.at[pl.ds(me * SRC_CAP, SRC_CAP), span],
            arrived[k].at[pl.ds(me * SRC_CAP, SRC_CAP)],
            local1.at[k],
        )

    for k in range(chunks):

        def far(j, carry, k=k):
            owner_copy(k, (1 - my_half) * half + (in_half + j) % half).start()
            return carry

        def near(j, carry, k=k):
            owner_copy(k, my_half * half + (in_half + j) % half).start()
            return carry

        lax.fori_loop(0, half, far, 0)
        lax.fori_loop(1, half, near, 0)
        own_copy(k).start()

    def own_step(c, carry):
        slot = slot_ref[source_ref[me * couplings + c]]
        owner = lax.div(slot, jnp.int32(pair_count))

        def block(i, first):
            for u in range(unroll):
                at = couplings - 1 - (i * unroll + u)
                other = slot_ref[source_ref[me * couplings + at]]
                same = lax.div(other, jnp.int32(pair_count)) == owner
                first = jnp.where(same, other, first)
            return first

        first = lax.fori_loop(0, couplings // unroll, block, slot)
        held_ref[c] = owner * SRC_CAP + jnp.where(first == slot, 0, 1)
        local_ref[c] = slot_ref[target_ref[me * couplings + c]] - base
        return carry

    lax.fori_loop(0, couplings, own_step, 0)

    def peer_copy(k, d):
        peer = (quarter + d) % quarters
        return pltpu.make_async_remote_copy(
            src_ref=picked.at[d - 1, k],
            dst_ref=whole.at[:, pl.ds(pl.multiple_of(quarter * rows + k * chunk_rows, 16), chunk_rows)],
            send_sem=send2.at[k, d],
            recv_sem=recv2.at[k, d],
            device_id=(me, peer),
            device_id_type=MESH,
        )

    def peer_arrival(k, d):
        peer = (quarter + quarters - d) % quarters
        return pltpu.make_async_remote_copy(
            src_ref=picked.at[d - 1, k],
            dst_ref=whole.at[:, pl.ds(pl.multiple_of(peer * rows + k * chunk_rows, 16), chunk_rows)],
            send_sem=send2.at[k, d],
            recv_sem=recv2.at[k, d],
            device_id=(me, peer),
            device_id_type=MESH,
        )

    for k in range(chunks):

        def take(j, carry, k=k):
            arrival(k, (me + j) % holders).wait_recv()
            return carry

        lax.fori_loop(1, holders, take, 0)
        own_copy(k).wait()
        for d in range(1, quarters):
            peer = (quarter + d) % quarters

            def pick(c, carry, k=k, d=d, peer=peer):
                picked[d - 1, k, c] = arrived[k][held_ref[peer * group + c]]
                return carry

            lax.fori_loop(0, group, pick, 0)

        for d in range(1, quarters):
            peer_copy(k, d).start()

        def keep(c, carry, k=k):
            start = pl.multiple_of(quarter * rows + k * chunk_rows, 16)
            whole[c, pl.ds(start, chunk_rows)] = arrived[k][held_ref[quarter * group + c]]
            return carry

        lax.fori_loop(0, group, keep, 0)

    for k in range(chunks):
        for d in range(1, quarters):
            peer_arrival(k, d).wait_recv()

    def term_copy(c, d):
        peer = (quarter + d) % quarters
        return pltpu.make_async_remote_copy(
            src_ref=sent_terms.at[c, pl.ds(pl.multiple_of(peer * rows, 16), rows)],
            dst_ref=terms_ref.at[quarter * group + c],
            send_sem=send3.at[c, d],
            recv_sem=recv3.at[c, d],
            device_id=(me, peer),
            device_id_type=MESH,
        )

    def term_arrival(c, d):
        peer = (quarter + quarters - d) % quarters
        return pltpu.make_async_remote_copy(
            src_ref=sent_terms.at[c, pl.ds(pl.multiple_of(peer * rows, 16), rows)],
            dst_ref=terms_ref.at[peer * group + c],
            send_sem=send3.at[c, d],
            recv_sem=recv3.at[c, d],
            device_id=(me, peer),
            device_id_type=MESH,
        )

    def own_term(c):
        return pltpu.make_async_copy(
            sent_terms.at[c, pl.ds(pl.multiple_of(quarter * rows, 16), rows)],
            terms_ref.at[quarter * group + c],
            local3.at[c],
        )

    def multiply(c, carry):
        inter_copy(c).wait()
        inter = inter_ref[c]
        left = jnp.dot(inter, whole[c], preferred_element_type=jnp.float32).astype(jnp.bfloat16)
        projected = lax.dot_general(
            left, inter, (((1,), (1,)), ((), ())), preferred_element_type=jnp.float32
        )
        sent_terms[c] = (fock_ref[c] * projected).astype(jnp.bfloat16)
        for d in range(1, quarters):
            term_copy(c, d).start()
        own_term(c).start()
        return carry

    lax.fori_loop(0, group, multiply, 0)

    def finish(c, carry):
        for d in range(1, quarters):
            term_arrival(c, d).wait_recv()
        for d in range(1, quarters):
            term_copy(c, d).wait_send()
        own_term(c).wait()
        return carry

    lax.fori_loop(0, group, finish, 0)
    for k in range(chunks):

        def sent(j, carry, k=k):
            owner_copy(k, (me + j) % holders).wait_send()
            return carry

        lax.fori_loop(1, holders, sent, 0)
        for d in range(1, quarters):
            peer_copy(k, d).wait_send()


def update_kernel(
    local_ref,
    gap_ref,
    terms_hbm,
    amp_hbm,
    integrals_hbm,
    energy_ref,
    new_hbm,
    residual_hbm,
    terms,
    amp,
    integrals,
    new,
    residual,
    columns,
    term_sem,
    in_sem,
    out_sem,
):
    quarter = lax.axis_index("dom")
    couplings = terms.shape[0]
    pair_count, rows, width = amp.shape

    def term_copy(c):
        return pltpu.make_async_copy(terms_hbm.at[c], terms.at[c], term_sem.at[c])

    def in_copies(p):
        return (
            pltpu.make_async_copy(amp_hbm.at[p], amp.at[p], in_sem.at[0, p]),
            pltpu.make_async_copy(integrals_hbm.at[p], integrals.at[p], in_sem.at[1, p]),
        )

    def out_copies(p):
        return (
            pltpu.make_async_copy(new.at[p], new_hbm.at[p], out_sem.at[0, p]),
            pltpu.make_async_copy(residual.at[p], residual_hbm.at[p], out_sem.at[1, p]),
        )

    def start_term(c, carry):
        term_copy(c).start()
        return carry

    lax.fori_loop(0, couplings, start_term, 0)
    for p in range(pair_count):
        for copy in in_copies(p):
            copy.start()
    columns[...] = jnp.transpose(energy_ref[...])
    residual[...] = jnp.zeros_like(residual)

    def add_term(c, carry):
        term_copy(c).wait()
        p = local_ref[c]
        residual[p] = residual[p] + terms[c].astype(jnp.float32)
        return carry

    lax.fori_loop(0, couplings, add_term, 0)
    own_rows = columns[pl.ds(pl.multiple_of(quarter * rows, 8), rows), :]
    for p in range(pair_count):
        for copy in in_copies(p):
            copy.wait()
        current = amp[p].astype(jnp.float32)
        denominator = own_rows[:, p : p + 1] + energy_ref[p : p + 1, :] + gap_ref[p]
        rest = integrals[p].astype(jnp.float32) + denominator * current - residual[p]
        residual[p] = rest
        new[p] = current - rest / denominator
        for copy in out_copies(p):
            copy.start()
    for p in range(pair_count):
        for copy in out_copies(p):
            copy.wait()


def per_device(
    amplitude,
    integrals,
    virtual_energy,
    occupied_gap,
    pair_slot,
    coupling_source,
    coupling_target,
    coupling_fock,
    coupling_intersection,
):
    holders = lax.axis_size("pairs")
    quarters = lax.axis_size("dom")
    own_quarter = lax.axis_index("dom")
    pair_count, rows, width = amplitude.shape
    couplings = coupling_source.shape[0] // holders
    group = coupling_intersection.shape[0]
    slots = holders * SRC_CAP
    chunk_rows = CHUNK_ROWS if rows % CHUNK_ROWS == 0 else rows
    chunks = rows // chunk_rows
    bf16 = jnp.bfloat16
    in_vmem = pl.BlockSpec(memory_space=VMEM)
    in_smem = pl.BlockSpec(memory_space=SMEM)
    anywhere = pl.BlockSpec(memory_space=pl.ANY)

    dma = pltpu.SemaphoreType.DMA
    terms, local = pl.pallas_call(
        functools.partial(exchange_kernel, holders, quarters),
        out_shape=(
            jax.ShapeDtypeStruct((couplings, rows, width), bf16),
            jax.ShapeDtypeStruct((couplings,), jnp.int32),
        ),
        in_specs=[in_smem, in_smem, in_smem, in_smem, in_vmem, anywhere],
        out_specs=(anywhere, in_smem),
        scratch_shapes=[
            VMEM((slots, rows, width), bf16),
            VMEM((group, quarters * rows, width), bf16),
            SMEM((couplings,), jnp.int32),
            dma((group,)),
            VMEM((group, quarters * rows, width), bf16),
            VMEM((quarters - 1, chunks, group, chunk_rows, width), bf16),
            VMEM((group, quarters * rows, width), bf16),
            dma((chunks, holders)),
            dma((chunks, holders)),
            dma((chunks,)),
            dma((chunks, quarters)),
            dma((chunks, quarters)),
            dma((group, quarters)),
            dma((group, quarters)),
            dma((group,)),
        ]
        + [VMEM((slots, chunk_rows, width), bf16)] * chunks,
        compiler_params=pltpu.CompilerParams(
            collective_id=0, has_side_effects=True, vmem_limit_bytes=60 << 20
        ),
        name="exchange",
    )(pair_slot, coupling_source, coupling_target, coupling_fock, amplitude, coupling_intersection)

    out = jax.ShapeDtypeStruct((pair_count, rows, width), jnp.float32)
    return pl.pallas_call(
        update_kernel,
        out_shape=(out, out),
        in_specs=[in_smem, in_smem, anywhere, anywhere, anywhere, in_vmem],
        out_specs=(anywhere, anywhere),
        scratch_shapes=[
            VMEM((couplings, rows, width), bf16),
            VMEM((pair_count, rows, width), bf16),
            VMEM((pair_count, rows, width), bf16),
            VMEM((pair_count, rows, width), jnp.float32),
            VMEM((pair_count, rows, width), jnp.float32),
            VMEM((width, pair_count), jnp.float32),
            dma((couplings,)),
            dma((2, pair_count)),
            dma((2, pair_count)),
        ],
        name="update",
    )(local, occupied_gap, terms, amplitude, integrals, virtual_energy)


def solution(mesh):
    in_specs = (
        P("pairs", "dom", None),
        P("pairs", "dom", None),
        P("pairs", None),
        P("pairs"),
        P(),
        P(),
        P(),
        P(("pairs", "dom")),
        P(("pairs", "dom"), None, None),
    )
    out_specs = (P("pairs", "dom", None), P("pairs", "dom", None))
    return jax.shard_map(
        per_device, mesh=mesh, in_specs=in_specs, out_specs=out_specs, check_vma=False
    )
```

```python
import functools

import jax
import jax.numpy as jnp
from jax import lax
from jax.experimental import pallas as pl
from jax.experimental.pallas import tpu as pltpu
from jax.sharding import PartitionSpec as P

SRC_CAP = 2
CHUNK_ROWS = 16
MESH = pl.DeviceIdType.MESH
VMEM = pltpu.VMEM
SMEM = pltpu.SMEM


def exchange_kernel(
    holders,
    quarters,
    slot_ref,
    source_ref,
    target_ref,
    fock_ref,
    amp_ref,
    inter_hbm,
    terms_ref,
    local_ref,
    out_ref,
    inter_ref,
    held_ref,
    inter_sem,
    whole,
    picked,
    sent_terms,
    send1,
    recv1,
    local1,
    send2,
    recv2,
    send3,
    recv3,
    local3,
    inter_x,
    fock_out,
    fock_in,
    half_terms,
    swap_send,
    swap_recv,
    half_send,
    half_recv,
    half_local,
    *arrived,
):
    me = lax.axis_index("pairs")
    quarter = lax.axis_index("dom")
    chunks = len(arrived)
    slots, chunk_rows, width = arrived[0].shape
    rows = chunk_rows * chunks
    group = inter_hbm.shape[0]
    half = holders // 2
    my_half = me // half
    in_half = me % half

    extra = whole.shape[0] - group
    full = group - extra
    partner = (quarter + quarters // 2) % quarters
    sibling = quarter + 1 - 2 * (quarter % 2)

    barrier = pltpu.get_barrier_semaphore()

    def greet(j, carry):
        pl.semaphore_signal(
            barrier, inc=1, device_id=((me + j) % holders, quarter), device_id_type=MESH
        )
        return carry

    lax.fori_loop(1, holders, greet, 0)
    for d in range(1, quarters):
        pl.semaphore_signal(
            barrier, inc=1, device_id=(me, (quarter + d) % quarters), device_id_type=MESH
        )

    def inter_copy(c):
        return pltpu.make_async_copy(inter_hbm.at[c], inter_ref.at[c], inter_sem.at[c])

    def fetch(c, carry):
        inter_copy(c).start()
        return carry

    lax.fori_loop(0, group, fetch, 0)

    pair_count = amp_ref.shape[0]
    couplings = source_ref.shape[0] // holders
    base = me * pair_count
    unroll = 8 if couplings % 8 == 0 else 1

    def holder_step(h, carry):
        def block(i, ab):
            first, second = ab
            for u in range(unroll):
                local = slot_ref[source_ref[h * couplings + i * unroll + u]] - base
                mine = (local >= 0) & (local < pair_count)
                free = first < 0
                second = jnp.where(mine & jnp.logical_not(free) & (local != first), local, second)
                first = jnp.where(mine & free, local, first)
            return first, second

        first, second = lax.fori_loop(
            0, couplings // unroll, block, (jnp.int32(-1), jnp.int32(-1))
        )
        out_ref[h * SRC_CAP] = amp_ref[jnp.maximum(first, 0)]
        out_ref[h * SRC_CAP + 1] = amp_ref[jnp.maximum(second, 0)]
        return carry

    fock_out[...] = jnp.full(fock_out.shape, fock_ref[group - 1], jnp.float32)
    lax.fori_loop(0, holders, holder_step, 0)
    pl.semaphore_wait(barrier, holders - 1 + quarters - 1)

    def swaps():
        for i, (src, dst) in enumerate(((inter_hbm.at[group - 1], inter_x), (fock_out, fock_in))):
            yield pltpu.make_async_remote_copy(
                src_ref=src,
                dst_ref=dst,
                send_sem=swap_send.at[i],
                recv_sem=swap_recv.at[i],
                device_id=(me, partner),
                device_id_type=MESH,
            )

    if extra:
        for copy in swaps():
            copy.start()

    def owner_copy(k, h):
        span = pl.ds(k * chunk_rows, chunk_rows)
        return pltpu.make_async_remote_copy(
            src_ref=out_ref.at[pl.ds(h * SRC_CAP, SRC_CAP), span],
            dst_ref=arrived[k].at[pl.ds(me * SRC_CAP, SRC_CAP)],
            send_sem=send1.at[k, h],
            recv_sem=recv1.at[k, me],
            device_id=(h, quarter),
            device_id_type=MESH,
        )

    def arrival(k, h):
        span = pl.ds(k * chunk_rows, chunk_rows)
        return pltpu.make_async_remote_copy(
            src_ref=out_ref.at[pl.ds(h * SRC_CAP, SRC_CAP), span],
            dst_ref=arrived[k].at[pl.ds(h * SRC_CAP, SRC_CAP)],
            send_sem=send1.at[k, h],
            recv_sem=recv1.at[k, h],
            device_id=(h, quarter),
            device_id_type=MESH,
        )

    def own_copy(k):
        span = pl.ds(k * chunk_rows, chunk_rows)
        return pltpu.make_async_copy(
            out_ref.at[pl.ds(me * SRC_CAP, SRC_CAP), span],
            arrived[k].at[pl.ds(me * SRC_CAP, SRC_CAP)],
            local1.at[k],
        )

    for k in range(chunks):

        def far(j, carry, k=k):
            owner_copy(k, (1 - my_half) * half + (in_half + j) % half).start()
            return carry

        def near(j, carry, k=k):
            owner_copy(k, my_half * half + (in_half + j) % half).start()
            return carry

        lax.fori_loop(0, half, far, 0)
        lax.fori_loop(1, half, near, 0)
        own_copy(k).start()

    def own_step(c, carry):
        slot = slot_ref[source_ref[me * couplings + c]]
        owner = lax.div(slot, jnp.int32(pair_count))

        def block(i, first):
            for u in range(unroll):
                at = couplings - 1 - (i * unroll + u)
                other = slot_ref[source_ref[me * couplings + at]]
                same = lax.div(other, jnp.int32(pair_count)) == owner
                first = jnp.where(same, other, first)
            return first

        first = lax.fori_loop(0, couplings // unroll, block, slot)
        held_ref[c] = owner * SRC_CAP + jnp.where(first == slot, 0, 1)
        local_ref[c] = slot_ref[target_ref[me * couplings + c]] - base
        return carry

    lax.fori_loop(0, couplings, own_step, 0)

    def peer_copy(k, d):
        peer = (quarter + d) % quarters
        return pltpu.make_async_remote_copy(
            src_ref=picked.at[d - 1, k],
            dst_ref=whole.at[:, pl.ds(pl.multiple_of(quarter * rows + k * chunk_rows, 16), chunk_rows)],
            send_sem=send2.at[k, d],
            recv_sem=recv2.at[k, d],
            device_id=(me, peer),
            device_id_type=MESH,
        )

    def peer_arrival(k, d):
        peer = (quarter + quarters - d) % quarters
        return pltpu.make_async_remote_copy(
            src_ref=picked.at[d - 1, k],
            dst_ref=whole.at[:, pl.ds(pl.multiple_of(peer * rows + k * chunk_rows, 16), chunk_rows)],
            send_sem=send2.at[k, d],
            recv_sem=recv2.at[k, d],
            device_id=(me, peer),
            device_id_type=MESH,
        )

    for k in range(chunks):

        def take(j, carry, k=k):
            arrival(k, (me + j) % holders).wait_recv()
            return carry

        lax.fori_loop(1, holders, take, 0)
        own_copy(k).wait()
        for d in range(1, quarters):
            peer = (quarter + d) % quarters

            def pick(c, carry, k=k, d=d, peer=peer):
                picked[d - 1, k, c] = arrived[k][held_ref[peer * group + c]]
                return carry

            lax.fori_loop(0, group, pick, 0)
            if extra:
                last = ((peer + quarters // 2) % quarters) * group + group - 1
                picked[d - 1, k, group] = arrived[k][held_ref[last]]

        for d in range(1, quarters):
            peer_copy(k, d).start()

        def keep(c, carry, k=k):
            start = pl.multiple_of(quarter * rows + k * chunk_rows, 16)
            whole[c, pl.ds(start, chunk_rows)] = arrived[k][held_ref[quarter * group + c]]
            return carry

        lax.fori_loop(0, group, keep, 0)
        if extra:
            start = pl.multiple_of(quarter * rows + k * chunk_rows, 16)
            last = partner * group + group - 1
            whole[group, pl.ds(start, chunk_rows)] = arrived[k][held_ref[last]]

    for k in range(chunks):
        for d in range(1, quarters):
            peer_arrival(k, d).wait_recv()

    def term_copy(c, d):
        peer = (quarter + d) % quarters
        return pltpu.make_async_remote_copy(
            src_ref=sent_terms.at[c, pl.ds(pl.multiple_of(peer * rows, 16), rows)],
            dst_ref=terms_ref.at[quarter * group + c],
            send_sem=send3.at[c, d],
            recv_sem=recv3.at[c, d],
            device_id=(me, peer),
            device_id_type=MESH,
        )

    def term_arrival(c, d):
        peer = (quarter + quarters - d) % quarters
        return pltpu.make_async_remote_copy(
            src_ref=sent_terms.at[c, pl.ds(pl.multiple_of(peer * rows, 16), rows)],
            dst_ref=terms_ref.at[peer * group + c],
            send_sem=send3.at[c, d],
            recv_sem=recv3.at[c, d],
            device_id=(me, peer),
            device_id_type=MESH,
        )

    def own_term(c):
        return pltpu.make_async_copy(
            sent_terms.at[c, pl.ds(pl.multiple_of(quarter * rows, 16), rows)],
            terms_ref.at[quarter * group + c],
            local3.at[c],
        )

    def multiply(c, carry):
        inter_copy(c).wait()
        inter = inter_ref[c]
        left = jnp.dot(inter, whole[c], preferred_element_type=jnp.float32).astype(jnp.bfloat16)
        projected = lax.dot_general(
            left, inter, (((1,), (1,)), ((), ())), preferred_element_type=jnp.float32
        )
        sent_terms[c] = (fock_ref[c] * projected).astype(jnp.bfloat16)
        for d in range(1, quarters):
            term_copy(c, d).start()
        own_term(c).start()
        return carry

    lax.fori_loop(0, full, multiply, 0)

    def half_copy(i):
        return pltpu.make_async_remote_copy(
            src_ref=half_terms.at[i, pl.ds(pl.multiple_of((sibling % 2) * rows, 16), rows)],
            dst_ref=terms_ref.at[(quarter, partner)[i] * group + group - 1],
            send_sem=half_send.at[i],
            recv_sem=half_recv.at[i],
            device_id=(me, sibling),
            device_id_type=MESH,
        )

    def half_arrival(i):
        owner = (sibling, (sibling + quarters // 2) % quarters)[i]
        return pltpu.make_async_remote_copy(
            src_ref=half_terms.at[i, pl.ds(pl.multiple_of((sibling % 2) * rows, 16), rows)],
            dst_ref=terms_ref.at[owner * group + group - 1],
            send_sem=half_send.at[i],
            recv_sem=half_recv.at[i],
            device_id=(me, sibling),
            device_id_type=MESH,
        )

    def half_own(i):
        return pltpu.make_async_copy(
            half_terms.at[i, pl.ds(pl.multiple_of((quarter % 2) * rows, 16), rows)],
            terms_ref.at[(quarter, partner)[i] * group + group - 1],
            half_local.at[i],
        )

    if extra:
        inter_copy(group - 1).wait()
        for copy in swaps():
            copy.wait_recv()
        own_half = pl.ds(pl.multiple_of((quarter // 2) * 2 * rows, 16), 2 * rows)
        for i in range(2):
            inter_i = inter_x if i else inter_ref.at[group - 1]
            scale = (fock_in if i else fock_out)[0:1, :]
            left = jnp.dot(
                inter_i[own_half, :], whole[group - 1 + i], preferred_element_type=jnp.float32
            ).astype(jnp.bfloat16)
            projected = lax.dot_general(
                left, inter_i[...], (((1,), (1,)), ((), ())), preferred_element_type=jnp.float32
            )
            half_terms[i] = (scale * projected).astype(jnp.bfloat16)
            half_copy(i).start()
            half_own(i).start()

    def finish(c, carry):
        for d in range(1, quarters):
            term_arrival(c, d).wait_recv()
        for d in range(1, quarters):
            term_copy(c, d).wait_send()
        own_term(c).wait()
        return carry

    lax.fori_loop(0, full, finish, 0)
    if extra:
        for i in range(2):
            half_arrival(i).wait_recv()
            half_copy(i).wait_send()
            half_own(i).wait()
        for copy in swaps():
            copy.wait_send()
    for k in range(chunks):

        def sent(j, carry, k=k):
            owner_copy(k, (me + j) % holders).wait_send()
            return carry

        lax.fori_loop(1, holders, sent, 0)
        for d in range(1, quarters):
            peer_copy(k, d).wait_send()


def update_kernel(
    local_ref,
    gap_ref,
    terms_hbm,
    amp_hbm,
    integrals_hbm,
    energy_ref,
    new_hbm,
    residual_hbm,
    terms,
    amp,
    integrals,
    new,
    residual,
    columns,
    term_sem,
    in_sem,
    out_sem,
):
    quarter = lax.axis_index("dom")
    couplings = terms.shape[0]
    pair_count, rows, width = amp.shape

    def term_copy(c):
        return pltpu.make_async_copy(terms_hbm.at[c], terms.at[c], term_sem.at[c])

    def in_copies(p):
        return (
            pltpu.make_async_copy(amp_hbm.at[p], amp.at[p], in_sem.at[0, p]),
            pltpu.make_async_copy(integrals_hbm.at[p], integrals.at[p], in_sem.at[1, p]),
        )

    def out_copies(p):
        return (
            pltpu.make_async_copy(new.at[p], new_hbm.at[p], out_sem.at[0, p]),
            pltpu.make_async_copy(residual.at[p], residual_hbm.at[p], out_sem.at[1, p]),
        )

    def start_term(c, carry):
        term_copy(c).start()
        return carry

    lax.fori_loop(0, couplings, start_term, 0)
    for p in range(pair_count):
        for copy in in_copies(p):
            copy.start()
    columns[...] = jnp.transpose(energy_ref[...])
    residual[...] = jnp.zeros_like(residual)

    def add_term(c, carry):
        term_copy(c).wait()
        p = local_ref[c]
        residual[p] = residual[p] + terms[c].astype(jnp.float32)
        return carry

    lax.fori_loop(0, couplings, add_term, 0)
    own_rows = columns[pl.ds(pl.multiple_of(quarter * rows, 8), rows), :]
    for p in range(pair_count):
        for copy in in_copies(p):
            copy.wait()
        current = amp[p].astype(jnp.float32)
        denominator = own_rows[:, p : p + 1] + energy_ref[p : p + 1, :] + gap_ref[p]
        rest = integrals[p].astype(jnp.float32) + denominator * current - residual[p]
        residual[p] = rest
        new[p] = current - rest / denominator
        for copy in out_copies(p):
            copy.start()
    for p in range(pair_count):
        for copy in out_copies(p):
            copy.wait()


def per_device(
    amplitude,
    integrals,
    virtual_energy,
    occupied_gap,
    pair_slot,
    coupling_source,
    coupling_target,
    coupling_fock,
    coupling_intersection,
):
    holders = lax.axis_size("pairs")
    quarters = lax.axis_size("dom")
    own_quarter = lax.axis_index("dom")
    pair_count, rows, width = amplitude.shape
    couplings = coupling_source.shape[0] // holders
    group = coupling_intersection.shape[0]
    slots = holders * SRC_CAP
    extra = 1 if quarters == 4 and group > 1 else 0
    chunk_rows = CHUNK_ROWS if rows % CHUNK_ROWS == 0 else rows
    chunks = rows // chunk_rows
    bf16 = jnp.bfloat16
    in_vmem = pl.BlockSpec(memory_space=VMEM)
    in_smem = pl.BlockSpec(memory_space=SMEM)
    anywhere = pl.BlockSpec(memory_space=pl.ANY)

    dma = pltpu.SemaphoreType.DMA
    terms, local = pl.pallas_call(
        functools.partial(exchange_kernel, holders, quarters),
        out_shape=(
            jax.ShapeDtypeStruct((couplings, rows, width), bf16),
            jax.ShapeDtypeStruct((couplings,), jnp.int32),
        ),
        in_specs=[in_smem, in_smem, in_smem, in_smem, in_vmem, anywhere],
        out_specs=(anywhere, in_smem),
        scratch_shapes=[
            VMEM((slots, rows, width), bf16),
            VMEM((group, quarters * rows, width), bf16),
            SMEM((couplings,), jnp.int32),
            dma((group,)),
            VMEM((group + extra, quarters * rows, width), bf16),
            VMEM((quarters - 1, chunks, group + extra, chunk_rows, width), bf16),
            VMEM((group, quarters * rows, width), bf16),
            dma((chunks, holders)),
            dma((chunks, holders)),
            dma((chunks,)),
            dma((chunks, quarters)),
            dma((chunks, quarters)),
            dma((group, quarters)),
            dma((group, quarters)),
            dma((group,)),
            VMEM((quarters * rows, width), bf16),
            VMEM((8, width), jnp.float32),
            VMEM((8, width), jnp.float32),
            VMEM((2, 2 * rows, width), bf16),
            dma((2,)),
            dma((2,)),
            dma((2,)),
            dma((2,)),
            dma((2,)),
        ]
        + [VMEM((slots, chunk_rows, width), bf16)] * chunks,
        compiler_params=pltpu.CompilerParams(
            collective_id=0, has_side_effects=True, vmem_limit_bytes=60 << 20
        ),
        name="exchange",
    )(pair_slot, coupling_source, coupling_target, coupling_fock, amplitude, coupling_intersection)

    out = jax.ShapeDtypeStruct((pair_count, rows, width), jnp.float32)
    return pl.pallas_call(
        update_kernel,
        out_shape=(out, out),
        in_specs=[in_smem, in_smem, anywhere, anywhere, anywhere, in_vmem],
        out_specs=(anywhere, anywhere),
        scratch_shapes=[
            VMEM((couplings, rows, width), bf16),
            VMEM((pair_count, rows, width), bf16),
            VMEM((pair_count, rows, width), bf16),
            VMEM((pair_count, rows, width), jnp.float32),
            VMEM((pair_count, rows, width), jnp.float32),
            VMEM((width, pair_count), jnp.float32),
            dma((couplings,)),
            dma((2, pair_count)),
            dma((2, pair_count)),
        ],
        name="update",
    )(local, occupied_gap, terms, amplitude, integrals, virtual_energy)


def solution(mesh):
    in_specs = (
        P("pairs", "dom", None),
        P("pairs", "dom", None),
        P("pairs", None),
        P("pairs"),
        P(),
        P(),
        P(),
        P(("pairs", "dom")),
        P(("pairs", "dom"), None, None),
    )
    out_specs = (P("pairs", "dom", None), P("pairs", "dom", None))
    return jax.shard_map(
        per_device, mesh=mesh, in_specs=in_specs, out_specs=out_specs, check_vma=False
    )
```

```python
import functools

import jax
import jax.numpy as jnp
from jax import lax
from jax.experimental import pallas as pl
from jax.experimental.pallas import tpu as pltpu
from jax.sharding import PartitionSpec as P

SRC_CAP = 2
CHUNK_ROWS = 16
MESH = pl.DeviceIdType.MESH
VMEM = pltpu.VMEM
SMEM = pltpu.SMEM


def exchange_kernel(
    holders,
    quarters,
    slot_ref,
    source_ref,
    target_ref,
    fock_ref,
    amp_hbm,
    inter_hbm,
    terms_ref,
    local_ref,
    out_ref,
    inter_ref,
    held_ref,
    inter_sem,
    amp_ref,
    amp_sem,
    whole,
    picked,
    sent_terms,
    send1,
    recv1,
    local1,
    send2,
    recv2,
    send3,
    recv3,
    local3,
    inter_x,
    fock_out,
    fock_in,
    half_terms,
    swap_send,
    swap_recv,
    half_send,
    half_recv,
    half_local,
    *arrived,
):
    amp_copy = pltpu.make_async_copy(amp_hbm, amp_ref, amp_sem)
    amp_copy.start()
    me = lax.axis_index("pairs")
    quarter = lax.axis_index("dom")
    chunks = len(arrived)
    slots, chunk_rows, width = arrived[0].shape
    rows = chunk_rows * chunks
    group = inter_hbm.shape[0]
    half = holders // 2
    my_half = me // half
    in_half = me % half

    extra = whole.shape[0] - group
    full = group - extra
    partner = (quarter + quarters // 2) % quarters
    sibling = quarter + 1 - 2 * (quarter % 2)

    barrier = pltpu.get_barrier_semaphore()

    def greet(j, carry):
        pl.semaphore_signal(
            barrier, inc=1, device_id=((me + j) % holders, quarter), device_id_type=MESH
        )
        return carry

    lax.fori_loop(1, holders, greet, 0)
    for d in range(1, quarters):
        pl.semaphore_signal(
            barrier, inc=1, device_id=(me, (quarter + d) % quarters), device_id_type=MESH
        )

    def inter_copy(c):
        return pltpu.make_async_copy(inter_hbm.at[c], inter_ref.at[c], inter_sem.at[c])

    def fetch(c, carry):
        inter_copy(c).start()
        return carry

    lax.fori_loop(0, group, fetch, 0)

    pair_count = amp_ref.shape[0]
    couplings = source_ref.shape[0] // holders
    base = me * pair_count
    unroll = 8 if couplings % 8 == 0 else 1

    def holder_step(h, carry):
        def block(i, ab):
            first, second = ab
            for u in range(unroll):
                local = slot_ref[source_ref[h * couplings + i * unroll + u]] - base
                mine = (local >= 0) & (local < pair_count)
                free = first < 0
                second = jnp.where(mine & jnp.logical_not(free) & (local != first), local, second)
                first = jnp.where(mine & free, local, first)
            return first, second

        first, second = lax.fori_loop(
            0, couplings // unroll, block, (jnp.int32(-1), jnp.int32(-1))
        )
        out_ref[h * SRC_CAP] = amp_ref[jnp.maximum(first, 0)]
        out_ref[h * SRC_CAP + 1] = amp_ref[jnp.maximum(second, 0)]
        return carry

    fock_out[...] = jnp.full(fock_out.shape, fock_ref[group - 1], jnp.float32)
    amp_copy.wait()
    lax.fori_loop(0, holders, holder_step, 0)
    pl.semaphore_wait(barrier, holders - 1 + quarters - 1)

    def swaps():
        for i, (src, dst) in enumerate(((inter_hbm.at[group - 1], inter_x), (fock_out, fock_in))):
            yield pltpu.make_async_remote_copy(
                src_ref=src,
                dst_ref=dst,
                send_sem=swap_send.at[i],
                recv_sem=swap_recv.at[i],
                device_id=(me, partner),
                device_id_type=MESH,
            )

    if extra:
        for copy in swaps():
            copy.start()

    def owner_copy(k, h):
        span = pl.ds(k * chunk_rows, chunk_rows)
        return pltpu.make_async_remote_copy(
            src_ref=out_ref.at[pl.ds(h * SRC_CAP, SRC_CAP), span],
            dst_ref=arrived[k].at[pl.ds(me * SRC_CAP, SRC_CAP)],
            send_sem=send1.at[k, h],
            recv_sem=recv1.at[k, me],
            device_id=(h, quarter),
            device_id_type=MESH,
        )

    def arrival(k, h):
        span = pl.ds(k * chunk_rows, chunk_rows)
        return pltpu.make_async_remote_copy(
            src_ref=out_ref.at[pl.ds(h * SRC_CAP, SRC_CAP), span],
            dst_ref=arrived[k].at[pl.ds(h * SRC_CAP, SRC_CAP)],
            send_sem=send1.at[k, h],
            recv_sem=recv1.at[k, h],
            device_id=(h, quarter),
            device_id_type=MESH,
        )

    def own_copy(k):
        span = pl.ds(k * chunk_rows, chunk_rows)
        return pltpu.make_async_copy(
            out_ref.at[pl.ds(me * SRC_CAP, SRC_CAP), span],
            arrived[k].at[pl.ds(me * SRC_CAP, SRC_CAP)],
            local1.at[k],
        )

    for k in range(chunks):

        def far(j, carry, k=k):
            owner_copy(k, (1 - my_half) * half + (in_half + j) % half).start()
            return carry

        def near(j, carry, k=k):
            owner_copy(k, my_half * half + (in_half + j) % half).start()
            return carry

        lax.fori_loop(0, half, far, 0)
        lax.fori_loop(1, half, near, 0)
        own_copy(k).start()

    def own_step(c, carry):
        slot = slot_ref[source_ref[me * couplings + c]]
        owner = lax.div(slot, jnp.int32(pair_count))

        def block(i, first):
            for u in range(unroll):
                at = couplings - 1 - (i * unroll + u)
                other = slot_ref[source_ref[me * couplings + at]]
                same = lax.div(other, jnp.int32(pair_count)) == owner
                first = jnp.where(same, other, first)
            return first

        first = lax.fori_loop(0, couplings // unroll, block, slot)
        held_ref[c] = owner * SRC_CAP + jnp.where(first == slot, 0, 1)
        local_ref[c] = slot_ref[target_ref[me * couplings + c]] - base
        return carry

    lax.fori_loop(0, couplings, own_step, 0)

    def peer_copy(k, d):
        peer = (quarter + d) % quarters
        return pltpu.make_async_remote_copy(
            src_ref=picked.at[d - 1, k],
            dst_ref=whole.at[:, pl.ds(pl.multiple_of(quarter * rows + k * chunk_rows, 16), chunk_rows)],
            send_sem=send2.at[k, d],
            recv_sem=recv2.at[k, d],
            device_id=(me, peer),
            device_id_type=MESH,
        )

    def peer_arrival(k, d):
        peer = (quarter + quarters - d) % quarters
        return pltpu.make_async_remote_copy(
            src_ref=picked.at[d - 1, k],
            dst_ref=whole.at[:, pl.ds(pl.multiple_of(peer * rows + k * chunk_rows, 16), chunk_rows)],
            send_sem=send2.at[k, d],
            recv_sem=recv2.at[k, d],
            device_id=(me, peer),
            device_id_type=MESH,
        )

    for k in range(chunks):

        def take(j, carry, k=k):
            arrival(k, (me + j) % holders).wait_recv()
            return carry

        lax.fori_loop(1, holders, take, 0)
        own_copy(k).wait()
        picked_all = []
        for d in sorted(range(1, quarters), key=lambda d: abs(2 * d - quarters)):
            peer = (quarter + d) % quarters

            def pick(c, carry, k=k, d=d, peer=peer):
                picked[d - 1, k, c] = arrived[k][held_ref[peer * group + c]]
                return carry

            lax.fori_loop(0, group, pick, 0)
            if extra:
                last = ((peer + quarters // 2) % quarters) * group + group - 1
                picked[d - 1, k, group] = arrived[k][held_ref[last]]
            picked_all.append(d)
            if len(picked_all) == quarters - 1:
                for e in picked_all:
                    peer_copy(k, e).start()

        def keep(c, carry, k=k):
            start = pl.multiple_of(quarter * rows + k * chunk_rows, 16)
            whole[c, pl.ds(start, chunk_rows)] = arrived[k][held_ref[quarter * group + c]]
            return carry

        lax.fori_loop(0, group, keep, 0)
        if extra:
            start = pl.multiple_of(quarter * rows + k * chunk_rows, 16)
            last = partner * group + group - 1
            whole[group, pl.ds(start, chunk_rows)] = arrived[k][held_ref[last]]

    for k in range(chunks):
        for d in range(1, quarters):
            peer_arrival(k, d).wait_recv()

    def term_copy(c, d):
        peer = (quarter + d) % quarters
        return pltpu.make_async_remote_copy(
            src_ref=sent_terms.at[c, pl.ds(pl.multiple_of(peer * rows, 16), rows)],
            dst_ref=terms_ref.at[quarter * group + c],
            send_sem=send3.at[c, d],
            recv_sem=recv3.at[c, d],
            device_id=(me, peer),
            device_id_type=MESH,
        )

    def term_arrival(c, d):
        peer = (quarter + quarters - d) % quarters
        return pltpu.make_async_remote_copy(
            src_ref=sent_terms.at[c, pl.ds(pl.multiple_of(peer * rows, 16), rows)],
            dst_ref=terms_ref.at[peer * group + c],
            send_sem=send3.at[c, d],
            recv_sem=recv3.at[c, d],
            device_id=(me, peer),
            device_id_type=MESH,
        )

    def own_term(c):
        return pltpu.make_async_copy(
            sent_terms.at[c, pl.ds(pl.multiple_of(quarter * rows, 16), rows)],
            terms_ref.at[quarter * group + c],
            local3.at[c],
        )

    def multiply(c, carry):
        inter_copy(c).wait()
        inter = inter_ref[c]
        left = jnp.dot(inter, whole[c], preferred_element_type=jnp.float32).astype(jnp.bfloat16)
        projected = lax.dot_general(
            left, inter, (((1,), (1,)), ((), ())), preferred_element_type=jnp.float32
        )
        sent_terms[c] = (fock_ref[c] * projected).astype(jnp.bfloat16)
        for d in range(1, quarters):
            term_copy(c, d).start()
        own_term(c).start()
        return carry

    lax.fori_loop(0, full, multiply, 0)

    def half_copy(i):
        return pltpu.make_async_remote_copy(
            src_ref=half_terms.at[i, pl.ds(pl.multiple_of((sibling % 2) * rows, 16), rows)],
            dst_ref=terms_ref.at[(quarter, partner)[i] * group + group - 1],
            send_sem=half_send.at[i],
            recv_sem=half_recv.at[i],
            device_id=(me, sibling),
            device_id_type=MESH,
        )

    def half_arrival(i):
        owner = (sibling, (sibling + quarters // 2) % quarters)[i]
        return pltpu.make_async_remote_copy(
            src_ref=half_terms.at[i, pl.ds(pl.multiple_of((sibling % 2) * rows, 16), rows)],
            dst_ref=terms_ref.at[owner * group + group - 1],
            send_sem=half_send.at[i],
            recv_sem=half_recv.at[i],
            device_id=(me, sibling),
            device_id_type=MESH,
        )

    def half_own(i):
        return pltpu.make_async_copy(
            half_terms.at[i, pl.ds(pl.multiple_of((quarter % 2) * rows, 16), rows)],
            terms_ref.at[(quarter, partner)[i] * group + group - 1],
            half_local.at[i],
        )

    if extra:
        inter_copy(group - 1).wait()
        for copy in swaps():
            copy.wait_recv()
        own_half = pl.ds(pl.multiple_of((quarter // 2) * 2 * rows, 16), 2 * rows)
        for i in range(2):
            inter_i = inter_x if i else inter_ref.at[group - 1]
            scale = (fock_in if i else fock_out)[0:1, :]
            left = jnp.dot(
                inter_i[own_half, :], whole[group - 1 + i], preferred_element_type=jnp.float32
            ).astype(jnp.bfloat16)
            projected = lax.dot_general(
                left, inter_i[...], (((1,), (1,)), ((), ())), preferred_element_type=jnp.float32
            )
            half_terms[i] = (scale * projected).astype(jnp.bfloat16)
            half_copy(i).start()
            half_own(i).start()

    def finish(c, carry):
        for d in range(1, quarters):
            term_arrival(c, d).wait_recv()
        for d in range(1, quarters):
            term_copy(c, d).wait_send()
        own_term(c).wait()
        return carry

    lax.fori_loop(0, full, finish, 0)
    if extra:
        for i in range(2):
            half_arrival(i).wait_recv()
            half_copy(i).wait_send()
            half_own(i).wait()
        for copy in swaps():
            copy.wait_send()
    for k in range(chunks):

        def sent(j, carry, k=k):
            owner_copy(k, (me + j) % holders).wait_send()
            return carry

        lax.fori_loop(1, holders, sent, 0)
        for d in range(1, quarters):
            peer_copy(k, d).wait_send()


def update_kernel(
    local_ref,
    gap_ref,
    terms_hbm,
    amp_hbm,
    integrals_hbm,
    energy_ref,
    new_hbm,
    residual_hbm,
    terms,
    amp,
    integrals,
    new,
    residual,
    columns,
    term_sem,
    in_sem,
    out_sem,
):
    quarter = lax.axis_index("dom")
    couplings = terms.shape[0]
    pair_count, rows, width = amp.shape

    def term_copy(c):
        return pltpu.make_async_copy(terms_hbm.at[c], terms.at[c], term_sem.at[c])

    def in_copies(p):
        return (
            pltpu.make_async_copy(amp_hbm.at[p], amp.at[p], in_sem.at[0, p]),
            pltpu.make_async_copy(integrals_hbm.at[p], integrals.at[p], in_sem.at[1, p]),
        )

    def out_copies(p):
        return (
            pltpu.make_async_copy(new.at[p], new_hbm.at[p], out_sem.at[0, p]),
            pltpu.make_async_copy(residual.at[p], residual_hbm.at[p], out_sem.at[1, p]),
        )

    def start_term(c, carry):
        term_copy(c).start()
        return carry

    for p in range(pair_count):
        for copy in in_copies(p):
            copy.start()
    lax.fori_loop(0, couplings, start_term, 0)
    columns[...] = jnp.transpose(energy_ref[...])
    own_rows = columns[pl.ds(pl.multiple_of(quarter * rows, 8), rows), :]

    def denominator(p):
        return own_rows[:, p : p + 1] + energy_ref[p : p + 1, :] + gap_ref[p]

    for p in range(pair_count):
        for copy in in_copies(p):
            copy.wait()
        current = amp[p].astype(jnp.float32)
        residual[p] = integrals[p].astype(jnp.float32) + denominator(p) * current

    def add_term(c, carry):
        term_copy(c).wait()
        p = local_ref[c]
        residual[p] = residual[p] - terms[c].astype(jnp.float32)
        return carry

    lax.fori_loop(0, couplings, add_term, 0)
    for p in range(pair_count):
        new[p] = amp[p].astype(jnp.float32) - residual[p] / denominator(p)
        for copy in out_copies(p):
            copy.start()
    for p in range(pair_count):
        for copy in out_copies(p):
            copy.wait()


def per_device(
    amplitude,
    integrals,
    virtual_energy,
    occupied_gap,
    pair_slot,
    coupling_source,
    coupling_target,
    coupling_fock,
    coupling_intersection,
):
    holders = lax.axis_size("pairs")
    quarters = lax.axis_size("dom")
    own_quarter = lax.axis_index("dom")
    pair_count, rows, width = amplitude.shape
    couplings = coupling_source.shape[0] // holders
    group = coupling_intersection.shape[0]
    slots = holders * SRC_CAP
    extra = 1 if quarters == 4 and group > 1 else 0
    chunk_rows = CHUNK_ROWS if rows % CHUNK_ROWS == 0 else rows
    chunks = rows // chunk_rows
    bf16 = jnp.bfloat16
    in_vmem = pl.BlockSpec(memory_space=VMEM)
    in_smem = pl.BlockSpec(memory_space=SMEM)
    anywhere = pl.BlockSpec(memory_space=pl.ANY)

    dma = pltpu.SemaphoreType.DMA
    terms, local = pl.pallas_call(
        functools.partial(exchange_kernel, holders, quarters),
        out_shape=(
            jax.ShapeDtypeStruct((couplings, rows, width), bf16),
            jax.ShapeDtypeStruct((couplings,), jnp.int32),
        ),
        in_specs=[in_smem, in_smem, in_smem, in_smem, anywhere, anywhere],
        out_specs=(anywhere, in_smem),
        scratch_shapes=[
            VMEM((slots, rows, width), bf16),
            VMEM((group, quarters * rows, width), bf16),
            SMEM((couplings,), jnp.int32),
            dma((group,)),
            VMEM((pair_count, rows, width), bf16),
            dma(()),
            VMEM((group + extra, quarters * rows, width), bf16),
            VMEM((quarters - 1, chunks, group + extra, chunk_rows, width), bf16),
            VMEM((group, quarters * rows, width), bf16),
            dma((chunks, holders)),
            dma((chunks, holders)),
            dma((chunks,)),
            dma((chunks, quarters)),
            dma((chunks, quarters)),
            dma((group, quarters)),
            dma((group, quarters)),
            dma((group,)),
            VMEM((quarters * rows, width), bf16),
            VMEM((8, width), jnp.float32),
            VMEM((8, width), jnp.float32),
            VMEM((2, 2 * rows, width), bf16),
            dma((2,)),
            dma((2,)),
            dma((2,)),
            dma((2,)),
            dma((2,)),
        ]
        + [VMEM((slots, chunk_rows, width), bf16)] * chunks,
        compiler_params=pltpu.CompilerParams(
            collective_id=0, has_side_effects=True, vmem_limit_bytes=60 << 20
        ),
        name="exchange",
    )(pair_slot, coupling_source, coupling_target, coupling_fock, amplitude, coupling_intersection)

    out = jax.ShapeDtypeStruct((pair_count, rows, width), jnp.float32)
    return pl.pallas_call(
        update_kernel,
        out_shape=(out, out),
        in_specs=[in_smem, in_smem, anywhere, anywhere, anywhere, in_vmem],
        out_specs=(anywhere, anywhere),
        scratch_shapes=[
            VMEM((couplings, rows, width), bf16),
            VMEM((pair_count, rows, width), bf16),
            VMEM((pair_count, rows, width), bf16),
            VMEM((pair_count, rows, width), jnp.float32),
            VMEM((pair_count, rows, width), jnp.float32),
            VMEM((width, pair_count), jnp.float32),
            dma((couplings,)),
            dma((2, pair_count)),
            dma((2, pair_count)),
        ],
        name="update",
    )(local, occupied_gap, terms, amplitude, integrals, virtual_energy)


def solution(mesh):
    in_specs = (
        P("pairs", "dom", None),
        P("pairs", "dom", None),
        P("pairs", None),
        P("pairs"),
        P(),
        P(),
        P(),
        P(("pairs", "dom")),
        P(("pairs", "dom"), None, None),
    )
    out_specs = (P("pairs", "dom", None), P("pairs", "dom", None))
    return jax.shard_map(
        per_device, mesh=mesh, in_specs=in_specs, out_specs=out_specs, check_vma=False
    )
```

```python
import functools

import jax
import jax.numpy as jnp
from jax import lax
from jax.experimental import pallas as pl
from jax.experimental.pallas import tpu as pltpu
from jax.sharding import PartitionSpec as P

SRC_CAP = 2
CHUNK_ROWS = 32
MESH = pl.DeviceIdType.MESH
VMEM = pltpu.VMEM
SMEM = pltpu.SMEM


def exchange_kernel(
    holders,
    quarters,
    slot_ref,
    source_ref,
    target_ref,
    fock_ref,
    amp_hbm,
    inter_hbm,
    terms_ref,
    local_ref,
    out_ref,
    inter_ref,
    held_ref,
    inter_sem,
    amp_ref,
    amp_sem,
    whole,
    picked,
    sent_terms,
    send1,
    recv1,
    local1,
    send2,
    recv2,
    send3,
    recv3,
    local3,
    inter_x,
    fock_out,
    fock_in,
    half_terms,
    swap_send,
    swap_recv,
    half_send,
    half_recv,
    half_local,
    *arrived,
):
    amp_copy = pltpu.make_async_copy(amp_hbm, amp_ref, amp_sem)
    amp_copy.start()
    me = lax.axis_index("pairs")
    quarter = lax.axis_index("dom")
    chunks = len(arrived)
    slots, chunk_rows, width = arrived[0].shape
    rows = chunk_rows * chunks
    group = inter_hbm.shape[0]
    half = holders // 2
    my_half = me // half
    in_half = me % half

    extra = whole.shape[0] - group
    full = group - extra
    partner = (quarter + quarters // 2) % quarters
    sibling = quarter + 1 - 2 * (quarter % 2)

    barrier = pltpu.get_barrier_semaphore()

    def greet(j, carry):
        pl.semaphore_signal(
            barrier, inc=1, device_id=((me + j) % holders, quarter), device_id_type=MESH
        )
        return carry

    lax.fori_loop(1, holders, greet, 0)
    for d in range(1, quarters):
        pl.semaphore_signal(
            barrier, inc=1, device_id=(me, (quarter + d) % quarters), device_id_type=MESH
        )

    def inter_copy(c):
        return pltpu.make_async_copy(inter_hbm.at[c], inter_ref.at[c], inter_sem.at[c])

    def fetch(c, carry):
        inter_copy(c).start()
        return carry

    lax.fori_loop(0, group, fetch, 0)

    pair_count = amp_ref.shape[0]
    couplings = source_ref.shape[0] // holders
    base = me * pair_count
    unroll = 8 if couplings % 8 == 0 else 1

    def holder_step(h, carry):
        def block(i, ab):
            first, second = ab
            for u in range(unroll):
                local = slot_ref[source_ref[h * couplings + i * unroll + u]] - base
                mine = (local >= 0) & (local < pair_count)
                free = first < 0
                second = jnp.where(mine & jnp.logical_not(free) & (local != first), local, second)
                first = jnp.where(mine & free, local, first)
            return first, second

        first, second = lax.fori_loop(
            0, couplings // unroll, block, (jnp.int32(-1), jnp.int32(-1))
        )
        out_ref[h * SRC_CAP] = amp_ref[jnp.maximum(first, 0)]
        out_ref[h * SRC_CAP + 1] = amp_ref[jnp.maximum(second, 0)]
        return carry

    fock_out[...] = jnp.full(fock_out.shape, fock_ref[group - 1], jnp.float32)
    amp_copy.wait()
    lax.fori_loop(0, holders, holder_step, 0)
    pl.semaphore_wait(barrier, holders - 1 + quarters - 1)

    def swaps():
        for i, (src, dst) in enumerate(((inter_hbm.at[group - 1], inter_x), (fock_out, fock_in))):
            yield pltpu.make_async_remote_copy(
                src_ref=src,
                dst_ref=dst,
                send_sem=swap_send.at[i],
                recv_sem=swap_recv.at[i],
                device_id=(me, partner),
                device_id_type=MESH,
            )

    if extra:
        for copy in swaps():
            copy.start()

    def owner_copy(k, h):
        span = pl.ds(k * chunk_rows, chunk_rows)
        return pltpu.make_async_remote_copy(
            src_ref=out_ref.at[pl.ds(h * SRC_CAP, SRC_CAP), span],
            dst_ref=arrived[k].at[pl.ds(me * SRC_CAP, SRC_CAP)],
            send_sem=send1.at[k, h],
            recv_sem=recv1.at[k, me],
            device_id=(h, quarter),
            device_id_type=MESH,
        )

    def arrival(k, h):
        span = pl.ds(k * chunk_rows, chunk_rows)
        return pltpu.make_async_remote_copy(
            src_ref=out_ref.at[pl.ds(h * SRC_CAP, SRC_CAP), span],
            dst_ref=arrived[k].at[pl.ds(h * SRC_CAP, SRC_CAP)],
            send_sem=send1.at[k, h],
            recv_sem=recv1.at[k, h],
            device_id=(h, quarter),
            device_id_type=MESH,
        )

    def own_copy(k):
        span = pl.ds(k * chunk_rows, chunk_rows)
        return pltpu.make_async_copy(
            out_ref.at[pl.ds(me * SRC_CAP, SRC_CAP), span],
            arrived[k].at[pl.ds(me * SRC_CAP, SRC_CAP)],
            local1.at[k],
        )

    for k in range(chunks):

        def far(j, carry, k=k):
            owner_copy(k, (1 - my_half) * half + (in_half + j) % half).start()
            return carry

        def near(j, carry, k=k):
            owner_copy(k, my_half * half + (in_half + j) % half).start()
            return carry

        lax.fori_loop(0, half, far, 0)
        lax.fori_loop(1, half, near, 0)
        own_copy(k).start()

    def own_step(c, carry):
        slot = slot_ref[source_ref[me * couplings + c]]
        owner = lax.div(slot, jnp.int32(pair_count))

        def block(i, first):
            for u in range(unroll):
                at = couplings - 1 - (i * unroll + u)
                other = slot_ref[source_ref[me * couplings + at]]
                same = lax.div(other, jnp.int32(pair_count)) == owner
                first = jnp.where(same, other, first)
            return first

        first = lax.fori_loop(0, couplings // unroll, block, slot)
        held_ref[c] = owner * SRC_CAP + jnp.where(first == slot, 0, 1)
        local_ref[c] = slot_ref[target_ref[me * couplings + c]] - base
        return carry

    lax.fori_loop(0, couplings, own_step, 0)

    def peer_copy(k, d):
        peer = (quarter + d) % quarters
        return pltpu.make_async_remote_copy(
            src_ref=picked.at[d - 1, k],
            dst_ref=whole.at[:, pl.ds(pl.multiple_of(quarter * rows + k * chunk_rows, 16), chunk_rows)],
            send_sem=send2.at[k, d],
            recv_sem=recv2.at[k, d],
            device_id=(me, peer),
            device_id_type=MESH,
        )

    def peer_arrival(k, d):
        peer = (quarter + quarters - d) % quarters
        return pltpu.make_async_remote_copy(
            src_ref=picked.at[d - 1, k],
            dst_ref=whole.at[:, pl.ds(pl.multiple_of(peer * rows + k * chunk_rows, 16), chunk_rows)],
            send_sem=send2.at[k, d],
            recv_sem=recv2.at[k, d],
            device_id=(me, peer),
            device_id_type=MESH,
        )

    for k in range(chunks):

        def take(j, carry, k=k):
            arrival(k, (me + j) % holders).wait_recv()
            return carry

        lax.fori_loop(1, holders, take, 0)
        own_copy(k).wait()
        picked_all = []
        for d in sorted(range(1, quarters), key=lambda d: abs(2 * d - quarters)):
            peer = (quarter + d) % quarters

            def pick(c, carry, k=k, d=d, peer=peer):
                picked[d - 1, k, c] = arrived[k][held_ref[peer * group + c]]
                return carry

            lax.fori_loop(0, group, pick, 0)
            if extra:
                last = ((peer + quarters // 2) % quarters) * group + group - 1
                picked[d - 1, k, group] = arrived[k][held_ref[last]]
            picked_all.append(d)
            if len(picked_all) == quarters - 1:
                for e in picked_all:
                    peer_copy(k, e).start()

        def keep(c, carry, k=k):
            start = pl.multiple_of(quarter * rows + k * chunk_rows, 16)
            whole[c, pl.ds(start, chunk_rows)] = arrived[k][held_ref[quarter * group + c]]
            return carry

        lax.fori_loop(0, group, keep, 0)
        if extra:
            start = pl.multiple_of(quarter * rows + k * chunk_rows, 16)
            last = partner * group + group - 1
            whole[group, pl.ds(start, chunk_rows)] = arrived[k][held_ref[last]]

    for k in range(chunks):
        for d in range(1, quarters):
            peer_arrival(k, d).wait_recv()

    def term_copy(c, d):
        peer = (quarter + d) % quarters
        return pltpu.make_async_remote_copy(
            src_ref=sent_terms.at[c, pl.ds(pl.multiple_of(peer * rows, 16), rows)],
            dst_ref=terms_ref.at[quarter * group + c],
            send_sem=send3.at[c, d],
            recv_sem=recv3.at[c, d],
            device_id=(me, peer),
            device_id_type=MESH,
        )

    def term_arrival(c, d):
        peer = (quarter + quarters - d) % quarters
        return pltpu.make_async_remote_copy(
            src_ref=sent_terms.at[c, pl.ds(pl.multiple_of(peer * rows, 16), rows)],
            dst_ref=terms_ref.at[peer * group + c],
            send_sem=send3.at[c, d],
            recv_sem=recv3.at[c, d],
            device_id=(me, peer),
            device_id_type=MESH,
        )

    def own_term(c):
        return pltpu.make_async_copy(
            sent_terms.at[c, pl.ds(pl.multiple_of(quarter * rows, 16), rows)],
            terms_ref.at[quarter * group + c],
            local3.at[c],
        )

    def multiply(c, carry):
        inter_copy(c).wait()
        inter = inter_ref[c]
        left = jnp.dot(inter, whole[c], preferred_element_type=jnp.float32).astype(jnp.bfloat16)
        projected = lax.dot_general(
            left, inter, (((1,), (1,)), ((), ())), preferred_element_type=jnp.float32
        )
        sent_terms[c] = (fock_ref[c] * projected).astype(jnp.bfloat16)
        for d in range(1, quarters):
            term_copy(c, d).start()
        own_term(c).start()
        return carry

    lax.fori_loop(0, full, multiply, 0)

    def half_copy(i):
        return pltpu.make_async_remote_copy(
            src_ref=half_terms.at[i, pl.ds(pl.multiple_of((sibling % 2) * rows, 16), rows)],
            dst_ref=terms_ref.at[(quarter, partner)[i] * group + group - 1],
            send_sem=half_send.at[i],
            recv_sem=half_recv.at[i],
            device_id=(me, sibling),
            device_id_type=MESH,
        )

    def half_arrival(i):
        owner = (sibling, (sibling + quarters // 2) % quarters)[i]
        return pltpu.make_async_remote_copy(
            src_ref=half_terms.at[i, pl.ds(pl.multiple_of((sibling % 2) * rows, 16), rows)],
            dst_ref=terms_ref.at[owner * group + group - 1],
            send_sem=half_send.at[i],
            recv_sem=half_recv.at[i],
            device_id=(me, sibling),
            device_id_type=MESH,
        )

    def half_own(i):
        return pltpu.make_async_copy(
            half_terms.at[i, pl.ds(pl.multiple_of((quarter % 2) * rows, 16), rows)],
            terms_ref.at[(quarter, partner)[i] * group + group - 1],
            half_local.at[i],
        )

    if extra:
        inter_copy(group - 1).wait()
        for copy in swaps():
            copy.wait_recv()
        own_half = pl.ds(pl.multiple_of((quarter // 2) * 2 * rows, 16), 2 * rows)
        for i in range(2):
            inter_i = inter_x if i else inter_ref.at[group - 1]
            scale = (fock_in if i else fock_out)[0:1, :]
            left = jnp.dot(
                inter_i[own_half, :], whole[group - 1 + i], preferred_element_type=jnp.float32
            ).astype(jnp.bfloat16)
            projected = lax.dot_general(
                left, inter_i[...], (((1,), (1,)), ((), ())), preferred_element_type=jnp.float32
            )
            half_terms[i] = (scale * projected).astype(jnp.bfloat16)
            half_copy(i).start()
            half_own(i).start()

    def finish(c, carry):
        for d in range(1, quarters):
            term_arrival(c, d).wait_recv()
        for d in range(1, quarters):
            term_copy(c, d).wait_send()
        own_term(c).wait()
        return carry

    lax.fori_loop(0, full, finish, 0)
    if extra:
        for i in range(2):
            half_arrival(i).wait_recv()
            half_copy(i).wait_send()
            half_own(i).wait()
        for copy in swaps():
            copy.wait_send()
    for k in range(chunks):

        def sent(j, carry, k=k):
            owner_copy(k, (me + j) % holders).wait_send()
            return carry

        lax.fori_loop(1, holders, sent, 0)
        for d in range(1, quarters):
            peer_copy(k, d).wait_send()


def update_kernel(
    local_ref,
    gap_ref,
    terms_hbm,
    amp_hbm,
    integrals_hbm,
    energy_ref,
    new_hbm,
    residual_hbm,
    terms,
    amp,
    integrals,
    new,
    residual,
    columns,
    term_sem,
    in_sem,
    out_sem,
):
    quarter = lax.axis_index("dom")
    couplings = terms.shape[0]
    pair_count, rows, width = amp.shape

    def term_copy(c):
        return pltpu.make_async_copy(terms_hbm.at[c], terms.at[c], term_sem.at[c])

    def in_copies(p):
        return (
            pltpu.make_async_copy(amp_hbm.at[p], amp.at[p], in_sem.at[0, p]),
            pltpu.make_async_copy(integrals_hbm.at[p], integrals.at[p], in_sem.at[1, p]),
        )

    def out_copies(p):
        return (
            pltpu.make_async_copy(new.at[p], new_hbm.at[p], out_sem.at[0, p]),
            pltpu.make_async_copy(residual.at[p], residual_hbm.at[p], out_sem.at[1, p]),
        )

    def start_term(c, carry):
        term_copy(c).start()
        return carry

    for p in range(pair_count):
        for copy in in_copies(p):
            copy.start()
    lax.fori_loop(0, couplings, start_term, 0)
    columns[...] = jnp.transpose(energy_ref[...])
    own_rows = columns[pl.ds(pl.multiple_of(quarter * rows, 8), rows), :]

    def denominator(p):
        return own_rows[:, p : p + 1] + energy_ref[p : p + 1, :] + gap_ref[p]

    for p in range(pair_count):
        for copy in in_copies(p):
            copy.wait()
        current = amp[p].astype(jnp.float32)
        residual[p] = integrals[p].astype(jnp.float32) + denominator(p) * current

    def add_term(c, carry):
        term_copy(c).wait()
        p = local_ref[c]
        residual[p] = residual[p] - terms[c].astype(jnp.float32)
        return carry

    lax.fori_loop(0, couplings, add_term, 0)
    for p in range(pair_count):
        new[p] = amp[p].astype(jnp.float32) - residual[p] / denominator(p)
        for copy in out_copies(p):
            copy.start()
    for p in range(pair_count):
        for copy in out_copies(p):
            copy.wait()


def per_device(
    amplitude,
    integrals,
    virtual_energy,
    occupied_gap,
    pair_slot,
    coupling_source,
    coupling_target,
    coupling_fock,
    coupling_intersection,
):
    holders = lax.axis_size("pairs")
    quarters = lax.axis_size("dom")
    own_quarter = lax.axis_index("dom")
    pair_count, rows, width = amplitude.shape
    couplings = coupling_source.shape[0] // holders
    group = coupling_intersection.shape[0]
    slots = holders * SRC_CAP
    extra = 1 if quarters == 4 and group > 1 else 0
    chunk_rows = CHUNK_ROWS if rows % CHUNK_ROWS == 0 else rows
    chunks = rows // chunk_rows
    bf16 = jnp.bfloat16
    in_vmem = pl.BlockSpec(memory_space=VMEM)
    in_smem = pl.BlockSpec(memory_space=SMEM)
    anywhere = pl.BlockSpec(memory_space=pl.ANY)

    dma = pltpu.SemaphoreType.DMA
    terms, local = pl.pallas_call(
        functools.partial(exchange_kernel, holders, quarters),
        out_shape=(
            jax.ShapeDtypeStruct((couplings, rows, width), bf16),
            jax.ShapeDtypeStruct((couplings,), jnp.int32),
        ),
        in_specs=[in_smem, in_smem, in_smem, in_smem, anywhere, anywhere],
        out_specs=(anywhere, in_smem),
        scratch_shapes=[
            VMEM((slots, rows, width), bf16),
            VMEM((group, quarters * rows, width), bf16),
            SMEM((couplings,), jnp.int32),
            dma((group,)),
            VMEM((pair_count, rows, width), bf16),
            dma(()),
            VMEM((group + extra, quarters * rows, width), bf16),
            VMEM((quarters - 1, chunks, group + extra, chunk_rows, width), bf16),
            VMEM((group, quarters * rows, width), bf16),
            dma((chunks, holders)),
            dma((chunks, holders)),
            dma((chunks,)),
            dma((chunks, quarters)),
            dma((chunks, quarters)),
            dma((group, quarters)),
            dma((group, quarters)),
            dma((group,)),
            VMEM((quarters * rows, width), bf16),
            VMEM((8, width), jnp.float32),
            VMEM((8, width), jnp.float32),
            VMEM((2, 2 * rows, width), bf16),
            dma((2,)),
            dma((2,)),
            dma((2,)),
            dma((2,)),
            dma((2,)),
        ]
        + [VMEM((slots, chunk_rows, width), bf16)] * chunks,
        compiler_params=pltpu.CompilerParams(
            collective_id=0, has_side_effects=True, vmem_limit_bytes=60 << 20
        ),
        name="exchange",
    )(pair_slot, coupling_source, coupling_target, coupling_fock, amplitude, coupling_intersection)

    out = jax.ShapeDtypeStruct((pair_count, rows, width), jnp.float32)
    return pl.pallas_call(
        update_kernel,
        out_shape=(out, out),
        in_specs=[in_smem, in_smem, anywhere, anywhere, anywhere, in_vmem],
        out_specs=(anywhere, anywhere),
        scratch_shapes=[
            VMEM((couplings, rows, width), bf16),
            VMEM((pair_count, rows, width), bf16),
            VMEM((pair_count, rows, width), bf16),
            VMEM((pair_count, rows, width), jnp.float32),
            VMEM((pair_count, rows, width), jnp.float32),
            VMEM((width, pair_count), jnp.float32),
            dma((couplings,)),
            dma((2, pair_count)),
            dma((2, pair_count)),
        ],
        name="update",
    )(local, occupied_gap, terms, amplitude, integrals, virtual_energy)


def solution(mesh):
    in_specs = (
        P("pairs", "dom", None),
        P("pairs", "dom", None),
        P("pairs", None),
        P("pairs"),
        P(),
        P(),
        P(),
        P(("pairs", "dom")),
        P(("pairs", "dom"), None, None),
    )
    out_specs = (P("pairs", "dom", None), P("pairs", "dom", None))
    return jax.shard_map(
        per_device, mesh=mesh, in_specs=in_specs, out_specs=out_specs, check_vma=False
    )
```
